256 devices in a mesh: ctx: 16 (over x_hi, y, core), exp: 16 (over z, x_lo).
Axes of the slice: x: 4 (x_hi: 2, x_lo: 2; x = x_hi * 2 + x_lo), y: 4, z: 8, core: 2. Of those that a mesh axis runs over, the one named last changes fastest.
Arguments:
- query: bfloat16 [1024, 8192], P('ctx', 'exp'), may hold values from -7 to 7
- keys: bfloat16 [32768, 512], P('ctx'), may hold values from -9 to 9
- values: bfloat16 [32768, 512], P('ctx'), may hold values from -6 to 6
- out_weight: bfloat16 [8192, 4096], P('exp'), may hold values from -3 to 3
- residual: bfloat16 [1024, 4096], P(('ctx', 'exp')), may hold values from -6 to 6
- norm_gain: float32 [4096], replicated, may hold values from 0.1 to 1.9
- expert_ids: int32 [1024, 8], P(('ctx', 'exp')), may hold values from 0 to 31, all different within a row; in each aligned block of 4 rows (0 to 3, 4 to 7, ...) at most 2 rows name the same one
- gate_values: float32 [1024, 8], P(('ctx', 'exp')), may hold values from 0.05 to 1
- w_gate_up: bfloat16 [32, 4096, 3072], P('exp', 'ctx'), may hold values from -0.09375 to 0.09375
- w_down: bfloat16 [32, 1536, 4096], P('exp', None, 'ctx'), may hold values from -0.15625 to 0.15625
Outputs:
- layer_out: float32 [1024, 4096], P(('ctx', 'exp'))
- head_max: float32 [64], P('exp')
The draws below stay inside these ranges and needn't reach their ends.
Inputs may be any that keep to these rules, and one draw needn't show every extreme that they name: `expert_ids`: each row names 8 different experts; in the rows of one device no expert is named more than 2 times.
All inputs are finite; a program needn't handle non-finite values.
Results may differ from the reference program's by a relative error of at most 0.018.
Values may be sent and summed in bfloat16 or wider, within the bound.
A program may use at most 192 MiB of HBM per device.

```python
import math
import jax
import jax.numpy as jnp
import numpy as np
from jax import lax

D = 4096
HEADS = 64
KVH = 4
HD = 128
FF = 1536
TOP = 8
EXPERTS = 32
L = 32768
Q = 1024
ROWS = 4
CAP = 2
SRC = 256
N_CTX = 16


def draw_query(key, part):
    base_key = jax.random.fold_in(key, 1)
    field = jnp.clip(jax.random.normal(base_key, (Q, HEADS * HD), jnp.float32), -6.0, 6.0)
    return field.astype(jnp.bfloat16)


def draw_keys(key, part):
    base_key = jax.random.fold_in(key, 2)
    field = jnp.clip(1.5 * jax.random.normal(base_key, (L, KVH * HD), jnp.float32), -8.5, 8.5)
    return field.astype(jnp.bfloat16)


def block_levels(own_key, shape, pieces, least, top_value):
    loudness, own = 1.0, jax.random.fold_in(own_key, 6)
    for position, shards_of in pieces:
        draws = jnp.exp(jax.random.uniform(jax.random.fold_in(own, position), (shards_of,), jnp.float32, least / len(pieces), top_value / len(pieces)))
        loudness = loudness * jnp.repeat(draws, shape[position] // shards_of).reshape([-1 if axis == position else 1 for axis in range(len(shape))])
    return loudness


def shared_out(rng, own, number, rows, count, top, bound, skew):
    order = jax.random.permutation(rng, count)
    packed, usual = load_shares(count, rows * top, bound, skew, True), load_shares(count, rows * top, bound, skew, False)
    places = jnp.arange(count)

    def named(sizes, turn):
        used = int((sizes > 0).sum())
        fixed = max(1, used // 4)
        shifted = fixed + (places - fixed + turn * (used - fixed)) % max(1, count - fixed)
        return jnp.zeros((count,), jnp.int32).at[order[jnp.where(places < fixed, places, shifted)]].set(jnp.asarray(sizes, jnp.int32))

    sizes = jnp.where(number % 4 == 0, named(packed, number // 4), named(usual, number - number // 4 - 1))
    mixed = jax.random.permutation(jax.random.fold_in(own, 3), count)
    donor, taker = mixed[0:count // 2 * 2:2], mixed[1:count // 2 * 2:2]
    slack = jnp.minimum(sizes[donor] - 1, bound - sizes[taker]) // 2
    slack = jnp.where((donor == order[0]) | (taker == order[0]) | (sizes[taker] == 0), 0, jnp.maximum(slack, 0))
    shifted = jax.random.randint(jax.random.fold_in(own, 4), (count // 2,), 0, 1 << 20) % (slack + 1)
    sizes = sizes.at[donor].add(-shifted).at[taker].add(shifted)
    labels = jnp.searchsorted(jnp.cumsum(sizes), jnp.arange(rows * top), side="right").astype(jnp.int32)
    listing = labels.reshape(top, rows).T
    listing = listing[jax.random.permutation(jax.random.fold_in(own, 1), rows)]
    turn = jax.random.randint(jax.random.fold_in(own, 2), (rows, 1), 0, top)
    return jnp.take_along_axis(listing, (jnp.arange(top)[None, :] + turn) % top, axis=1)


def load_shares(count, total, bound, lean, full):
    loads = [(1 << 20) // math.isqrt(standing ** lean) + 1 for standing in range(1, count + 1)]
    largest = bound if full else min(bound, max(-(-total // count), total * loads[0] // sum(loads)))
    least = 1 if total - largest >= count - 1 else 0
    given, rest = [largest] + [least] * (count - 1), total - largest - least * (count - 1)
    while rest > 0:
        movable = [i for i in range(1, count) if given[i] < largest] or [i for i in range(1, count) if given[i] < bound]
        mass, budget = sum([loads[i] for i in movable]), rest
        for i in movable:
            extra = min(bound - given[i], max(1, budget * loads[i] // mass), rest)
            given[i] = given[i] + extra
            rest = rest - extra
    return np.array(given)


def noise(key, extent, scale, bound, pieces=(), kind=jnp.bfloat16):
    drawn = scale * jax.random.normal(key, extent, jnp.float32)
    if pieces:
        drawn = drawn * block_levels(key, extent, pieces, -0.22, 0.18)
    return jnp.clip(drawn, -bound, bound).astype(kind)


def setup_inputs(seed: int = 0) -> dict:
    key_of = jax.random.split(jax.random.key(seed), 11)
    query = draw_query(jax.random.fold_in(key_of[10], 71), 0)
    keys = draw_keys(jax.random.fold_in(key_of[10], 71), 0)
    values = noise(key_of[2], (L, KVH * HD), 1.0, 6.0, ((0, 16),))
    out_weight = noise(key_of[3], (HEADS * HD, D), 0.5, 3.0, ((0, 16),))
    residual = noise(key_of[4], (Q, D), 1.0, 6.0, ((0, 256),))
    norm_gain = jnp.clip(1.0 + 0.18 * jax.random.normal(key_of[5], (D,), jnp.float32), 0.1, 1.9)
    expert_ids_keys = jax.random.split(jax.random.fold_in(key_of[6], 1), Q // ROWS)
    expert_ids_turns = jax.random.permutation(jax.random.fold_in(key_of[6], 3), Q // ROWS)
    expert_ids = jax.vmap(lambda own, number: shared_out(jax.random.fold_in(key_of[6], 2), own, number, ROWS, EXPERTS, TOP, CAP, 2))(expert_ids_keys, expert_ids_turns).reshape((Q, TOP))
    gate_values = jnp.clip(jnp.exp(math.log(1.0) - 2.9957323 * jax.random.uniform(key_of[7], (Q, TOP), jnp.float32) ** block_levels(key_of[7], (Q, TOP), ((0, 256),), -0.2, 0.2)), 0.05, 1.0)
    w_gate_up = noise(key_of[8], (EXPERTS, D, 2 * FF), D ** -0.5, 0.09375, ((0, 16), (1, 16)))
    w_down = noise(key_of[9], (EXPERTS, FF, D), FF ** -0.5, 0.15625, ((0, 16), (2, 16)))
    return {"query": query, "keys": keys, "values": values, "out_weight": out_weight, "residual": residual, "norm_gain": norm_gain, "expert_ids": expert_ids, "gate_values": gate_values, "w_gate_up": w_gate_up, "w_down": w_down}


eps = 1e-06

def reference(query, keys, values, out_weight, residual, norm_gain, expert_ids, gate_values, w_gate_up, w_down):
    length = keys.shape[0]
    row_count = query.shape[0]
    group_size = HEADS // KVH
    score_scale = 1.0 / math.sqrt(HD)
    q_all = query.reshape(row_count, HEADS, HD)
    k_all = keys.reshape(length, KVH, HD)
    v_all = values.reshape(length, KVH, HD)
    q_pos = (length - row_count + jnp.arange(row_count)).astype(jnp.int32)
    k_pos = jnp.arange(length).astype(jnp.int32)
    visible = k_pos[None, :] <= q_pos[:, None]

    def one_head(head_index):
        kv_index = head_index // group_size
        q_head = lax.dynamic_index_in_dim(q_all, head_index, 1, keepdims=False)
        k_head = lax.dynamic_index_in_dim(k_all, kv_index, 1, keepdims=False)
        v_head = lax.dynamic_index_in_dim(v_all, kv_index, 1, keepdims=False)
        scores = jnp.dot(q_head, k_head.T, preferred_element_type=jnp.float32) * score_scale
        scores = jnp.where(visible, scores, -jnp.inf)
        row_peak = lax.optimization_barrier(jnp.max(scores, axis=1))
        weights = jnp.exp(scores - row_peak[:, None])
        row_total = lax.optimization_barrier(jnp.sum(weights, axis=1))
        mixed_rows = jnp.dot(weights.astype(jnp.bfloat16), v_head, preferred_element_type=jnp.float32)
        return ((mixed_rows / row_total[:, None]).astype(jnp.bfloat16), jnp.max(row_peak))
    heads_out, head_max = lax.map(one_head, jnp.arange(HEADS, dtype=jnp.int32))
    attended = heads_out.transpose(1, 0, 2).reshape(row_count, HEADS * HD)
    state_rows = residual.astype(jnp.float32) + jnp.dot(attended, out_weight, preferred_element_type=jnp.float32)
    normed = (state_rows * lax.rsqrt(lax.optimization_barrier(jnp.mean(state_rows * state_rows, axis=1, keepdims=True)) + eps) * norm_gain).astype(jnp.bfloat16)
    feature_blocks = normed.reshape(row_count, N_CTX, D // N_CTX)
    bound_rows = SRC * CAP

    def add_expert(carry_sum, expert):
        named_here = expert_ids == expert
        row_weight = lax.optimization_barrier(jnp.sum(jnp.where(named_here, gate_values, 0.0), axis=1))
        chosen = jnp.any(named_here, axis=1)
        picked = jnp.nonzero(chosen, size=bound_rows, fill_value=0)[0]
        live_rows = (jnp.arange(bound_rows) < jnp.sum(chosen.astype(jnp.int32))).astype(jnp.float32)
        x_rows = feature_blocks[picked].astype(jnp.float32)
        w_in = lax.dynamic_index_in_dim(w_gate_up, expert, 0, keepdims=False).reshape(N_CTX, D // N_CTX, 2 * FF)
        partial_value = jnp.einsum('mcd,cdf->mcf', x_rows, w_in.astype(jnp.float32))
        rounded = lax.optimization_barrier(partial_value.astype(jnp.bfloat16))
        summed = lax.optimization_barrier(jnp.sum(rounded.astype(jnp.float32), axis=1))
        inner_units = (jax.nn.silu(summed[:, :FF]) * summed[:, FF:]).astype(jnp.bfloat16)
        w_out = lax.dynamic_index_in_dim(w_down, expert, 0, keepdims=False)
        out_rows = jnp.dot(inner_units, w_out, preferred_element_type=jnp.float32).astype(jnp.bfloat16)
        out_rows = lax.optimization_barrier(out_rows).astype(jnp.float32)
        contrib = (row_weight[picked] * live_rows)[:, None] * out_rows
        return (carry_sum.at[picked].add(contrib), None)
    moe_sum, unused = lax.scan(add_expert, jnp.zeros((row_count, D), jnp.float32), jnp.arange(EXPERTS, dtype=jnp.int32))
    layer_out = state_rows + moe_sum
    return (layer_out, head_max)
```

```python
import functools
import math

import jax
import jax.numpy as jnp
from jax import lax
from jax.experimental import pallas as pl
from jax.experimental.pallas import tpu as pltpu
from jax.sharding import PartitionSpec as P

HEADS = 64
KVH = 4
HD = 128
EPS = 1e-06
NEG = -1e30
MESH = pl.DeviceIdType.MESH
ANY = pl.BlockSpec(memory_space=pl.ANY)
VM = pl.BlockSpec(memory_space=pltpu.VMEM)
F32 = jnp.float32
BF16 = jnp.bfloat16
DMA = pltpu.SemaphoreType.DMA


def loop(n, body, start=0):
    def step(i, carry):
        body(i)
        return carry

    lax.fori_loop(start, n, step, 0)


def place(cn, en):
    return lax.axis_index("ctx"), lax.axis_index("exp")


def greet(targets):
    barrier = pltpu.get_barrier_semaphore()
    total = 0
    for first, last, device in targets:
        loop(
            last,
            lambda j, device=device: pl.semaphore_signal(
                barrier, inc=1, device_id=device(j), device_id_type=MESH
            ),
            start=first,
        )
        total += last - first
    pl.semaphore_wait(barrier, total)


def remote(src, dst, send, recv, device):
    return pltpu.make_async_remote_copy(
        src_ref=src,
        dst_ref=dst,
        send_sem=send,
        recv_sem=recv,
        device_id=device,
        device_id_type=MESH,
    )


def attend_kernel(cn, en, q, keys, vals, w, o, st, wother, qbuf, kbuf, vbuf, vt, sbuf, mbuf,
                  qs, qr, ws, wr, ls):
    c, e = place(cn, en)
    h = lax.rem(c, 2)
    other = c + 1 - 2 * h
    rows, width = q.shape
    heads = width // HD
    key_rows = keys.shape[0]
    half = w.shape[2] // 4
    kv = pl.multiple_of((e * heads // (HEADS // KVH)) * HD, HD)
    kcopy = pltpu.make_async_copy(keys.at[:, pl.ds(kv, HD)], kbuf, ls.at[0])
    vcopy = pltpu.make_async_copy(vals.at[:, pl.ds(kv, HD)], vbuf, ls.at[1])
    qcopy = pltpu.make_async_copy(q, qbuf.at[c], ls.at[2])
    kcopy.start()
    vcopy.start()
    qcopy.start()
    greet([(1, cn, lambda j: (lax.rem(c + j, cn), e))])

    def push(j):
        return remote(q, qbuf.at[c], qs.at[j], qr.at[c], (lax.rem(c + j, cn), e))

    loop(cn, lambda j: push(j).start(), start=1)

    def wpush(part):
        off = pl.multiple_of(part * 2 * half + (1 - h) * half, 128)
        return remote(
            w.at[:, :, pl.ds(off, half)],
            wother.at[:, :, pl.ds(part * half, half)],
            ws.at[part],
            wr.at[part],
            (other, e),
        )

    wpush(0).start()
    wpush(1).start()
    kcopy.wait()
    vcopy.wait()
    qcopy.wait()
    vt[...] = vbuf[...].astype(F32).T.astype(BF16)
    mbuf[...] = jnp.full(mbuf.shape, NEG, F32)
    cols = heads * rows
    scale = 1.0 / math.sqrt(HD)
    scale2 = scale * math.log2(math.e)
    first_q = key_rows * cn - rows * cn
    kc = min(512, key_rows)

    def one(j):
        cs = lax.rem(c + cn - j, cn)

        @pl.when(j > 0)
        def _():
            remote(q, qbuf.at[cs], qs.at[0], qr.at[cs], (cs, e)).wait_recv()

        qv = qbuf[cs]
        qcat = jnp.concatenate([qv[:, i * HD : (i + 1) * HD] for i in range(heads)], axis=0)
        for t in range(key_rows // kc):
            sbuf[t * kc : (t + 1) * kc, :] = lax.dot_general(
                kbuf[t * kc : (t + 1) * kc, :],
                qcat,
                (((1,), (1,)), ((), ())),
                preferred_element_type=F32,
            )

        @pl.when(c == cn - 1)
        def _():
            lane = lax.rem(lax.broadcasted_iota(jnp.int32, (1, cols), 1), rows)
            limit = first_q + cs * rows + lane - c * key_rows
            for t in range(key_rows // kc):
                kpos = t * kc + lax.broadcasted_iota(jnp.int32, (kc, cols), 0)
                sbuf[t * kc : (t + 1) * kc, :] = jnp.where(
                    kpos <= limit, sbuf[t * kc : (t + 1) * kc, :], NEG
                )

        m = jnp.max(sbuf[0:kc, :], axis=0, keepdims=True)
        for t in range(1, key_rows // kc):
            m = jnp.maximum(m, jnp.max(sbuf[t * kc : (t + 1) * kc, :], axis=0, keepdims=True))
        total = jnp.zeros((1, cols), F32)
        acc = jnp.zeros((HD, cols), F32)
        for t in range(key_rows // kc):
            p = jnp.exp2((sbuf[t * kc : (t + 1) * kc, :] - m) * scale2)
            total = total + jnp.sum(p, axis=0, keepdims=True)
            acc = acc + jnp.dot(
                vt[:, t * kc : (t + 1) * kc], p.astype(BF16), preferred_element_type=F32
            )
        out = acc.T.astype(BF16)
        for i in range(heads):
            o[cs, :, i * HD : (i + 1) * HD] = out[i * rows : (i + 1) * rows, :]
        ms = m * scale
        hc = cols // 2
        st[cs, 0:1, :hc] = ms[:, :hc]
        st[cs, 1:2, :hc] = ms[:, hc:]
        st[cs, 2:3, :hc] = total[:, :hc]
        st[cs, 3:4, :hc] = total[:, hc:]
        mbuf[0:1, :] = jnp.maximum(mbuf[0:1, :], ms)

    loop(cn, one)
    hc = cols // 2

    def spread(j):
        st[j, 4:5, :hc] = mbuf[0:1, :hc]
        st[j, 5:6, :hc] = mbuf[0:1, hc:]

    loop(cn, spread)
    loop(cn, lambda j: push(j).wait_send(), start=1)
    wpush(0).wait()
    wpush(1).wait()


def project_kernel(cn, en, o, st, w, out, hm, obuf, stbuf, wbuf, coef, a2, os_, or_, ss, sr, ls):
    c, e = place(cn, en)
    rows, width = o.shape[1:]
    heads = width // HD
    wcopy = pltpu.make_async_copy(w, wbuf, ls.at[0])
    ocopy = pltpu.make_async_copy(o.at[c], obuf.at[c], ls.at[1])
    scopy = pltpu.make_async_copy(st.at[c], stbuf.at[c], ls.at[2])
    wcopy.start()
    ocopy.start()
    scopy.start()
    greet([(1, cn, lambda j: (lax.rem(c + j, cn), e))])

    def opush(j):
        c2 = lax.rem(c + j, cn)
        return remote(o.at[c2], obuf.at[c], os_.at[j], or_.at[c], (c2, e))

    def spush(j):
        c2 = lax.rem(c + j, cn)
        return remote(st.at[c2], stbuf.at[c], ss.at[j], sr.at[c], (c2, e))

    def begin(j):
        spush(j).start()
        opush(j).start()

    def arrive(j):
        c2 = lax.rem(c + cn - j, cn)
        remote(st.at[c2], stbuf.at[c2], ss.at[j], sr.at[c2], (c2, e)).wait_recv()
        remote(o.at[c2], obuf.at[c2], os_.at[j], or_.at[c2], (c2, e)).wait_recv()

    loop(cn, begin, start=1)
    ocopy.wait()
    scopy.wait()
    loop(cn, arrive, start=1)
    stats = [stbuf[i] for i in range(cn)]
    top = functools.reduce(jnp.maximum, stats)
    hm[...] = top
    peak = top[0:2, :]
    weights = [jnp.exp(s[0:2, :] - peak) for s in stats]
    total = sum(wt * s[2:4, :] for wt, s in zip(weights, stats))
    coef[...] = jnp.zeros(coef.shape, F32)
    for i in range(cn):
        coef[2 * i : 2 * i + 2, :] = weights[i] / total
    turned = coef[...].T
    dup = (
        lax.broadcasted_iota(jnp.int32, (2 * rows, rows), 1)
        == lax.broadcasted_iota(jnp.int32, (2 * rows, rows), 0) // 8 * 4
        + lax.rem(lax.broadcasted_iota(jnp.int32, (2 * rows, rows), 0), 4)
    ).astype(BF16)
    for i in range(heads):
        lo = (i % (heads // 2)) * rows
        acc = jnp.zeros((rows, HD), F32)
        for k in range(cn):
            acc = acc + turned[lo : lo + rows, 2 * k + i // (heads // 2) : 2 * k + i // (heads // 2) + 1] * obuf[
                k, :, i * HD : (i + 1) * HD
            ].astype(F32)
        a2[:, i * HD : (i + 1) * HD] = jnp.dot(
            dup, acc.astype(BF16), preferred_element_type=F32
        ).astype(BF16)
    wcopy.wait()
    left = a2[...]
    n = out.shape[2]
    nc = min(256, n)
    low = lax.rem(lax.broadcasted_iota(jnp.int32, (2 * rows, nc), 0), 8) < 4

    def column(t):
        at = pl.multiple_of(t * nc, nc)
        r0 = jnp.dot(left, wbuf[:, pl.ds(at, nc)], preferred_element_type=F32)
        r1 = jnp.dot(left, wbuf[:, pl.ds(at + n, nc)], preferred_element_type=F32)
        r = jnp.where(low, r0, r1)
        for k in range(en):
            out[k, :, pl.ds(at, nc)] = r[8 * k : 8 * k + 8, :].astype(BF16)

    loop(n // nc, column)
    loop(cn, lambda j: opush(j).wait_send(), start=1)
    loop(cn, lambda j: spush(j).wait_send(), start=1)


def norm_kernel(cn, en, p, gm, residual, gain, state, x, gp, pbuf, gbuf, ps, pr, gs, gr, ls):
    c, e = place(cn, en)
    pcopy = pltpu.make_async_copy(p.at[e], pbuf.at[e], ls.at[0])
    gcopy = pltpu.make_async_copy(gm.at[e], gbuf.at[e], ls.at[1])
    pcopy.start()
    gcopy.start()
    greet([(1, en, lambda j: (c, lax.rem(e + j, en)))])

    def ppush(j):
        e2 = lax.rem(e + j, en)
        return remote(p.at[e2], pbuf.at[e], ps.at[j], pr.at[e], (c, e2))

    def gpush(j):
        e2 = lax.rem(e + j, en)
        return remote(gm.at[e2], gbuf.at[e], gs.at[j], gr.at[e], (c, e2))

    def begin(j):
        ppush(j).start()
        gpush(j).start()

    def arrive(j):
        e2 = lax.rem(e + en - j, en)
        remote(p.at[e2], pbuf.at[e2], ps.at[j], pr.at[e2], (c, e2)).wait_recv()
        remote(gm.at[e2], gbuf.at[e2], gs.at[j], gr.at[e2], (c, e2)).wait_recv()

    loop(en, begin, start=1)
    pcopy.wait()
    gcopy.wait()
    loop(en, arrive, start=1)
    gp[...] = sum(gbuf[i] for i in range(en))
    s = sum(pbuf[i].astype(F32) for i in range(en))
    n = s.shape[1]
    s0 = s[0:4, :] + residual[:, :n].astype(F32)
    s1 = s[4:8, :] + residual[:, n:].astype(F32)
    state[:, :n] = s0
    state[:, n:] = s1
    mean = (
        jnp.sum(s0 * s0, axis=1, keepdims=True) + jnp.sum(s1 * s1, axis=1, keepdims=True)
    ) * (1.0 / (2 * n))
    scale = lax.rsqrt(mean + EPS)
    n0 = s0 * scale * gain[:, :n]
    n1 = s1 * scale * gain[:, n:]
    for i in range(cn):
        part, off = (n0, i * 256) if i * 256 < n else (n1, i * 256 - n)
        x[i] = jnp.concatenate(
            [part[:, off : off + 128], part[:, off + 128 : off + 256]], axis=0
        ).astype(BF16)
    loop(en, lambda j: ppush(j).wait_send(), start=1)
    loop(en, lambda j: gpush(j).wait_send(), start=1)


def slot_gates(cn, gall, group):
    lanes = 8 * cn
    row = lax.broadcasted_iota(jnp.int32, (lanes, lanes), 0)
    col = lax.broadcasted_iota(jnp.int32, (lanes, lanes), 1)
    k = lax.broadcasted_iota(jnp.int32, (128, lanes), 0)
    which = lax.rem(lax.broadcasted_iota(jnp.int32, (128, lanes), 1) // cn, 4)
    pick = (k == 4 * group + which).astype(F32)
    spread = jnp.dot(gall, pick, preferred_element_type=F32, precision=lax.Precision.HIGHEST)
    same = row // 8 == lax.rem(col, cn)
    same_half = lax.rem(row // 4, 2) == col // (4 * cn)
    return spread, same, same_half


def expert_kernel(cn, en, x, gp, w, wother, y, gall, mid, gbuf, xbuf, wbuf, xs,
                  ms, mr, gs, gr, es, er, ps, pr, ls):
    c, e = place(cn, en)
    h = lax.rem(c, 2)
    other = c + 1 - 2 * h
    half = w.shape[2] // 4
    copies = [
        pltpu.make_async_copy(
            w.at[:, :, pl.ds(pl.multiple_of(part * 2 * half + h * half, 128), half)],
            wbuf.at[:, h, :, pl.ds(part * half, half)],
            ls.at[part],
        )
        for part in range(2)
    ]
    copies.append(pltpu.make_async_copy(wother, wbuf.at[:, 1 - h], ls.at[2]))
    xcopy = pltpu.make_async_copy(x.at[c], mid.at[c], ls.at[3])
    gcopy = pltpu.make_async_copy(gp, gbuf.at[c], ls.at[4])
    for copy in copies + [xcopy, gcopy]:
        copy.start()
    greet([
        (1, cn, lambda j: (lax.rem(c + j, cn), e)),
        (1, en, lambda j: (c, lax.rem(e + j, en))),
    ])

    def mpush(j):
        c2 = lax.rem(c + j, cn)
        return remote(x.at[c2], mid.at[c], ms.at[j], mr.at[c], (c2, e))

    def gpush(j):
        return remote(gp, gbuf.at[c], gs.at[j], gr.at[c], (lax.rem(c + j, cn), e))

    def begin(j):
        mpush(j).start()
        gpush(j).start()

    def arrive(j):
        c2 = lax.rem(c + cn - j, cn)
        remote(x.at[c2], mid.at[c2], ms.at[j], mr.at[c2], (c2, e)).wait_recv()

    loop(cn, begin, start=1)
    xcopy.wait()
    loop(cn, arrive, start=1)

    def epush(j):
        return remote(mid, xbuf.at[h, e], es.at[j], er.at[e], (c, lax.rem(e + j, en)))

    loop(en, lambda j: epush(j).start(), start=1)
    ecopy = pltpu.make_async_copy(mid, xbuf.at[h, e], ls.at[5])
    ecopy.start()
    ecopy.wait()

    def ppush(j):
        e2 = lax.rem(e + en - j, en)
        return remote(xbuf.at[h, e2], xbuf.at[h, e2], ps.at[e2], pr.at[e2], (other, e))

    ppush(0).start()

    def relay(j):
        e2 = lax.rem(e + en - j, en)
        remote(mid, xbuf.at[h, e2], es.at[j], er.at[e2], (c, e2)).wait_recv()
        ppush(j).start()

    loop(en, relay, start=1)
    gcopy.wait()

    def garrive(j):
        c2 = lax.rem(c + cn - j, cn)
        remote(gp, gbuf.at[c2], gs.at[j], gr.at[c2], (c2, e)).wait_recv()

    loop(cn, garrive, start=1)

    def parrive(e2):
        remote(
            xbuf.at[1 - h, e2], xbuf.at[1 - h, e2], ps.at[e2], pr.at[e2], (other, e)
        ).wait_recv()

    loop(en, parrive)
    lanes = 8 * cn
    rows = gbuf[...].reshape(lanes, 128)
    gall[...] = rows

    def group(g):
        spread, same, same_half = slot_gates(cn, rows, g)
        one = jnp.where(same & same_half & (spread > 0.0), 1.0, 0.0).astype(BF16)
        at = pl.multiple_of(g * 2 * cn, 2 * cn)
        for core in range(2):
            xv = xbuf[core, g].astype(F32).reshape(lanes, 128).astype(BF16)
            r = lax.dot_general(
                one, xv, (((0,), (0,)), ((), ())), preferred_element_type=F32
            ).astype(BF16)
            for hf in range(2):
                for k in range(2):
                    lo = hf * 4 * cn + k * 2 * cn
                    f = core * 256 + hf * 128
                    xs[k, pl.ds(at, 2 * cn), f : f + 128] = r[lo : lo + 2 * cn, :]

    loop(en, group)
    for copy in copies:
        copy.wait()
    nchunk = y.shape[0] // 2
    crow = y.shape[1]
    nc = min(256, 2 * half)
    for k in range(2):
        def column(t, k=k):
            at = pl.multiple_of(t * nc, nc)
            r = jnp.dot(xs[k, :, 0:256], wbuf[k, 0, :, pl.ds(at, nc)], preferred_element_type=F32)
            r = r + jnp.dot(
                xs[k, :, 256:512], wbuf[k, 1, :, pl.ds(at, nc)], preferred_element_type=F32
            )
            r = r.astype(BF16)
            for i in range(nchunk):
                y[k * nchunk + i, :, pl.ds(at, nc)] = r[i * crow : (i + 1) * crow, :]

        loop(2 * half // nc, column)
    loop(cn, lambda j: mpush(j).wait_send(), start=1)
    loop(cn, lambda j: gpush(j).wait_send(), start=1)
    loop(en, lambda j: epush(j).wait_send(), start=1)
    loop(en, lambda j: ppush(j).wait_send())


def hidden_kernel(cn, en, y, hid, ybuf, ys, yr, ls):
    c, e = place(cn, en)
    h = lax.rem(c, 2)
    nk = cn // 2
    chip = c // 2
    copy = pltpu.make_async_copy(y.at[chip], ybuf.at[chip], ls.at[0])
    copy.start()
    greet([(1, nk, lambda j: (lax.rem(chip + j, nk) * 2 + h, e))])

    def push(j):
        k = lax.rem(chip + j, nk)
        return remote(y.at[k], ybuf.at[chip], ys.at[j], yr.at[chip], (k * 2 + h, e))

    def arrive(j):
        k = lax.rem(chip + nk - j, nk)
        remote(y.at[k], ybuf.at[k], ys.at[j], yr.at[k], (k * 2 + h, e)).wait_recv()

    loop(nk, lambda j: push(j).start(), start=1)
    copy.wait()
    loop(nk, arrive, start=1)
    half = hid.shape[1]
    rc = 16

    def block(t):
        at = pl.multiple_of(t * rc, rc)
        gate = sum(ybuf[k, pl.ds(at, rc), 0:half].astype(F32) for k in range(nk))
        up = sum(ybuf[k, pl.ds(at, rc), half:].astype(F32) for k in range(nk))
        hid[pl.ds(at, rc), :] = (gate / (1.0 + jnp.exp(-gate)) * up).astype(BF16)

    loop(hid.shape[0] // rc, block)
    loop(nk, lambda j: push(j).wait_send(), start=1)


def down_kernel(cn, en, hid, wd, gall, comb, hbuf, wbuf, obuf, hs, hr, ps, pr, ls):
    c, e = place(cn, en)
    h = lax.rem(c, 2)
    other = c + 1 - 2 * h
    nk = cn // 2
    chip = c // 2
    wcopy = pltpu.make_async_copy(wd, wbuf, ls.at[0])
    hcopy = pltpu.make_async_copy(hid, hbuf.at[h, chip], ls.at[1])
    wcopy.start()
    hcopy.start()
    greet([
        (1, nk, lambda j: (lax.rem(chip + j, nk) * 2 + h, e)),
        (0, 1, lambda j: (other, e)),
    ])

    def push(j):
        k = lax.rem(chip + j, nk)
        return remote(hid, hbuf.at[h, chip], hs.at[j], hr.at[chip], (k * 2 + h, e))

    def ppush(j):
        k = lax.rem(chip + nk - j, nk)
        return remote(hbuf.at[h, k], hbuf.at[h, k], ps.at[k], pr.at[k], (other, e))

    loop(nk, lambda j: push(j).start(), start=1)
    hcopy.wait()
    ppush(0).start()

    def relay(j):
        k = lax.rem(chip + nk - j, nk)
        remote(hid, hbuf.at[h, k], hs.at[j], hr.at[k], (k * 2 + h, e)).wait_recv()
        ppush(j).start()

    loop(nk, relay, start=1)

    def parrive(k):
        remote(
            hbuf.at[1 - h, k], hbuf.at[1 - h, k], ps.at[k], pr.at[k], (other, e)
        ).wait_recv()

    loop(nk, parrive)
    wcopy.wait()
    half = hid.shape[1]
    crow = hid.shape[0]
    each = nk // 2

    def down(k):
        x = k // each
        r = jnp.dot(hbuf[0, k], wbuf[x, 0:half, :], preferred_element_type=F32)
        r = r + jnp.dot(hbuf[1, k], wbuf[x, half:, :], preferred_element_type=F32)
        obuf[x, pl.ds(pl.multiple_of(lax.rem(k, each) * crow, crow), crow), :] = r.astype(BF16)

    loop(nk, down)
    rows = gall[...]
    lanes = 8 * cn
    low = lax.rem(lax.broadcasted_iota(jnp.int32, (lanes, 128), 0), 8) < 4

    def group(g):
        spread, same, same_half = slot_gates(cn, rows, g)
        gates = jnp.where(same, spread, 0.0)[:, : 4 * cn]
        hi = gates.astype(BF16)
        lo = (gates - hi.astype(F32)).astype(BF16)
        at = pl.multiple_of(g * 2 * cn, 2 * cn)
        ov = jnp.concatenate(
            [obuf[0, pl.ds(at, 2 * cn), :], obuf[1, pl.ds(at, 2 * cn), :]], axis=0
        )
        r = jnp.dot(hi, ov, preferred_element_type=F32)
        r = r + jnp.dot(lo, ov, preferred_element_type=F32)
        comb[g] = jnp.where(low, r[:, :128], r[:, 128:]).reshape(cn, 8, 128).astype(BF16)

    loop(en, group)
    loop(nk, lambda j: push(j).wait_send(), start=1)
    loop(nk, lambda j: ppush(j).wait_send())


def return_kernel(cn, en, comb, state, out, r1, r2, es, er, cs, cr, ls):
    c, e = place(cn, en)
    ecopy = pltpu.make_async_copy(comb.at[e], r1.at[e], ls.at[0])
    ecopy.start()
    greet([
        (1, cn, lambda j: (lax.rem(c + j, cn), e)),
        (1, en, lambda j: (c, lax.rem(e + j, en))),
    ])

    def epush(j):
        e2 = lax.rem(e + j, en)
        return remote(comb.at[e2], r1.at[e], es.at[j], er.at[e], (c, e2))

    def earrive(j):
        e2 = lax.rem(e + en - j, en)
        remote(comb.at[e2], r1.at[e2], es.at[j], er.at[e2], (c, e2)).wait_recv()

    loop(en, lambda j: epush(j).start(), start=1)
    ecopy.wait()
    loop(en, earrive, start=1)

    def cpush(j):
        c2 = lax.rem(c + j, cn)
        return remote(r1.at[:, c2], r2.at[c], cs.at[j], cr.at[c], (c2, e))

    def carrive(j):
        c2 = lax.rem(c + cn - j, cn)
        remote(r1.at[:, c2], r2.at[c2], cs.at[j], cr.at[c2], (c2, e)).wait_recv()

    loop(cn, lambda j: cpush(j).start(), start=1)
    ccopy = pltpu.make_async_copy(r1.at[:, c], r2.at[c], ls.at[1])
    ccopy.start()
    ccopy.wait()
    loop(cn, carrive, start=1)
    for i in range(cn):
        s = sum(r2[i, k].astype(F32) for k in range(en))
        for hf in range(2):
            f = i * 256 + hf * 128
            out[:, f : f + 128] = state[:, f : f + 128] + s[4 * hf : 4 * hf + 4, :]
    loop(en, lambda j: epush(j).wait_send(), start=1)
    loop(cn, lambda j: cpush(j).wait_send(), start=1)


def call(body, cn, en, ident, ins, outs, scratch, args):
    return pl.pallas_call(
        functools.partial(body, cn, en),
        out_shape=tuple(jax.ShapeDtypeStruct(s, d) for s, d, _ in outs),
        in_specs=list(ins),
        out_specs=tuple(b for _, _, b in outs),
        scratch_shapes=scratch,
        compiler_params=pltpu.CompilerParams(
            collective_id=ident, has_side_effects=True, vmem_limit_bytes=60 << 20
        ),
        name=body.__name__,
    )(*args)


def gate_blocks(en, expert_ids, gate_values):
    rows = expert_ids.shape[0]
    experts = 2 * en
    hit = expert_ids[:, :, None] == jnp.arange(experts, dtype=jnp.int32)
    dense = jnp.sum(jnp.where(hit, gate_values[:, :, None], 0.0), axis=1)
    named = jnp.any(hit, axis=1).astype(jnp.int32)
    rank = jnp.cumsum(named, axis=0) - named
    ranked = jnp.where(
        rank[:, :, None] == jnp.arange(2, dtype=jnp.int32), dense[:, :, None], 0.0
    )
    blocks = ranked.reshape(rows, en, 4).transpose(1, 0, 2)
    blocks = jnp.concatenate([blocks, blocks], axis=1)
    mine = lax.axis_index("exp")
    spot = jnp.arange(128, dtype=jnp.int32) // 4 == mine
    return jnp.where(spot, jnp.tile(blocks, (1, 1, 32)), 0.0)


def local(cn, en, query, keys, values, out_weight, residual, norm_gain, expert_ids, gate_values,
          w_gate_up, w_down):
    rows, width = query.shape
    d = out_weight.shape[1]
    key_rows = keys.shape[0]
    cols = rows * (width // HD)
    ff = w_down.shape[1]
    half = ff // 2
    fb = w_gate_up.shape[1]
    nk = cn // 2
    slots = 2 * cn * en
    crow = 2 * slots // nk
    gm = gate_blocks(en, expert_ids, gate_values)
    o, st, wother = call(
        attend_kernel, cn, en, 0, [ANY] * 4,
        [((cn, rows, width), BF16, VM), ((cn, 8, 128), F32, VM), ((2, fb, ff), BF16, ANY)],
        [
            pltpu.VMEM((cn, rows, width), BF16),
            pltpu.VMEM((key_rows, HD), BF16),
            pltpu.VMEM((key_rows, HD), BF16),
            pltpu.VMEM((HD, key_rows), BF16),
            pltpu.VMEM((key_rows, cols), F32),
            pltpu.VMEM((8, cols), F32),
            DMA((cn,)), DMA((cn,)), DMA((2,)), DMA((2,)), DMA((3,)),
        ],
        (query, keys, values, w_gate_up),
    )
    p, hm = call(
        project_kernel, cn, en, 1, [ANY] * 3,
        [((en, 8, d // 2), BF16, VM), ((8, 128), F32, VM)],
        [
            pltpu.VMEM((cn, rows, width), BF16),
            pltpu.VMEM((cn, 8, 128), F32),
            pltpu.VMEM((width, d), BF16),
            pltpu.VMEM((128, 128), F32),
            pltpu.VMEM((2 * rows, width), BF16),
            DMA((cn,)), DMA((cn,)), DMA((cn,)), DMA((cn,)), DMA((3,)),
        ],
        (o, st, out_weight),
    )
    state, x, gp = call(
        norm_kernel, cn, en, 2, [ANY, ANY, VM, VM],
        [((4, d), F32, VM), ((cn, 8, 128), BF16, VM), ((8, 128), F32, VM)],
        [
            pltpu.VMEM((en, 8, d // 2), BF16),
            pltpu.VMEM((en, 8, 128), F32),
            DMA((en,)), DMA((en,)), DMA((en,)), DMA((en,)), DMA((2,)),
        ],
        (p, gm, residual, norm_gain.reshape(1, d)),
    )
    y, gall = call(
        expert_kernel, cn, en, 3, [ANY] * 4,
        [((nk, crow, ff), BF16, VM), ((8 * cn, 128), F32, VM)],
        [
            pltpu.VMEM((cn, 8, 128), BF16),
            pltpu.VMEM((cn, 8, 128), F32),
            pltpu.VMEM((2, en, cn, 8, 128), BF16),
            pltpu.VMEM((2, 2, fb, ff), BF16),
            pltpu.VMEM((2, slots, 2 * fb), BF16),
            DMA((cn,)), DMA((cn,)), DMA((cn,)), DMA((cn,)),
            DMA((en,)), DMA((en,)), DMA((en,)), DMA((en,)), DMA((6,)),
        ],
        (x, gp, w_gate_up, wother),
    )
    (hid,) = call(
        hidden_kernel, cn, en, 4, [ANY],
        [((crow, half), BF16, VM)],
        [pltpu.VMEM((nk, crow, ff), BF16), DMA((nk,)), DMA((nk,)), DMA((1,))],
        (y,),
    )
    (comb,) = call(
        down_kernel, cn, en, 5, [ANY, ANY, VM],
        [((en, cn, 8, 128), BF16, VM)],
        [
            pltpu.VMEM((2, nk, crow, half), BF16),
            pltpu.VMEM((2, ff, fb), BF16),
            pltpu.VMEM((2, slots, fb), BF16),
            DMA((nk,)), DMA((nk,)), DMA((nk,)), DMA((nk,)), DMA((2,)),
        ],
        (hid, w_down, gall),
    )
    (layer_out,) = call(
        return_kernel, cn, en, 6, [ANY, VM],
        [((4, d), F32, VM)],
        [
            pltpu.VMEM((en, cn, 8, 128), BF16),
            pltpu.VMEM((cn, en, 8, 128), BF16),
            DMA((en,)), DMA((en,)), DMA((cn,)), DMA((cn,)), DMA((2,)),
        ],
        (comb, state),
    )
    heads = width // HD
    head_max = jnp.max(hm[4:6, : cols // 2].reshape(heads, rows), axis=1)
    return layer_out, head_max


def solution(mesh):
    cn, en = mesh.shape["ctx"], mesh.shape["exp"]
    return jax.shard_map(
        functools.partial(local, cn, en),
        mesh=mesh,
        in_specs=(
            P("ctx", "exp"),
            P("ctx", None),
            P("ctx", None),
            P("exp", None),
            P(("ctx", "exp"), None),
            P(),
            P(("ctx", "exp"), None),
            P(("ctx", "exp"), None),
            P("exp", "ctx", None),
            P("exp", None, "ctx"),
        ),
        out_specs=(P(("ctx", "exp"), None), P("exp")),
        check_vma=False,
    )
```

```python
import functools
import math

import jax
import jax.numpy as jnp
from jax import lax
from jax.experimental import pallas as pl
from jax.experimental.pallas import tpu as pltpu
from jax.sharding import PartitionSpec as P

HEADS = 64
KVH = 4
HD = 128
EPS = 1e-06
NEG = -1e30
MESH = pl.DeviceIdType.MESH
ANY = pl.BlockSpec(memory_space=pl.ANY)
VM = pl.BlockSpec(memory_space=pltpu.VMEM)
F32 = jnp.float32
BF16 = jnp.bfloat16
DMA = pltpu.SemaphoreType.DMA


def loop(n, body, start=0):
    def step(i, carry):
        body(i)
        return carry

    lax.fori_loop(start, n, step, 0)


def place(cn, en):
    return lax.axis_index("ctx"), lax.axis_index("exp")


def greet(targets):
    barrier = pltpu.get_barrier_semaphore()
    total = 0
    for first, last, device in targets:
        loop(
            last,
            lambda j, device=device: pl.semaphore_signal(
                barrier, inc=1, device_id=device(j), device_id_type=MESH
            ),
            start=first,
        )
        total += last - first
    pl.semaphore_wait(barrier, total)


def remote(src, dst, send, recv, device):
    return pltpu.make_async_remote_copy(
        src_ref=src,
        dst_ref=dst,
        send_sem=send,
        recv_sem=recv,
        device_id=device,
        device_id_type=MESH,
    )


def slot_gates(cn, gall, group):
    lanes = 8 * cn
    row = lax.broadcasted_iota(jnp.int32, (lanes, lanes), 0)
    col = lax.broadcasted_iota(jnp.int32, (lanes, lanes), 1)
    k = lax.broadcasted_iota(jnp.int32, (128, lanes), 0)
    which = lax.rem(lax.broadcasted_iota(jnp.int32, (128, lanes), 1) // cn, 4)
    pick = (k == 4 * group + which).astype(F32)
    spread = jnp.dot(gall, pick, preferred_element_type=F32, precision=lax.Precision.HIGHEST)
    same = row // 8 == lax.rem(col, cn)
    same_half = lax.rem(row // 4, 2) == col // (4 * cn)
    return spread, same, same_half


def layer_kernel(cn, en, q, keys, vals, w, outw, wd, ids, gates, residual, gain, out, hm,
                 qbuf, kbuf, vbuf, vt, sbuf, mbuf, osend, obuf, stsend, stbuf, hmsend, hmbuf,
                 gsend, gbuf, gpsend, gall, owbuf, coef, a2, psend, pbuf, state, xsend, mid, xbuf,
                 wbuf, slotm, gatem, xs, ysend, ybuf, hbuf, wdbuf, csend, r1, r2,
                 qs, qr, os_, or_, ss, sr, ms, mr, gs, gr, gps, gpr, ws, wr, ps, pr, xsm, xrm,
                 es, er, es2, er2, ys, yr, hs, hr, hs2, hr2, cs_, cr_, rs_, rr_, ls):
    c, e = place(cn, en)
    h = lax.rem(c, 2)
    other = c + 1 - 2 * h
    chip = c // 2
    nk = cn // 2
    gq = cn // 4
    nq = en // gq
    rows, width = q.shape
    heads = width // HD
    key_rows = keys.shape[0]
    half = w.shape[2] // 4
    cols = heads * rows
    hc = cols // 2
    lanes = 8 * cn
    d = outw.shape[1]
    n = d // 2

    def ctx(j):
        return (lax.rem(c + j, cn), e)

    def exp(j):
        return (c, lax.rem(e + j, en))

    def csrc(j):
        return lax.rem(c + cn - j, cn)

    def esrc(j):
        return lax.rem(e + en - j, en)

    kv = pl.multiple_of((e * heads // (HEADS // KVH)) * HD, HD)
    kcopy = pltpu.make_async_copy(keys.at[:, pl.ds(kv, HD)], kbuf, ls.at[0])
    vcopy = pltpu.make_async_copy(vals.at[:, pl.ds(kv, HD)], vbuf, ls.at[1])
    qcopy = pltpu.make_async_copy(q, qbuf.at[c], ls.at[2])
    owcopy = pltpu.make_async_copy(outw, owbuf, ls.at[3])
    wdcopy = pltpu.make_async_copy(wd, wdbuf, ls.at[4])
    wcopies = [
        pltpu.make_async_copy(
            w.at[:, :, pl.ds(pl.multiple_of(part * 2 * half + h * half, 128), half)],
            wbuf.at[:, h, :, pl.ds(part * half, half)],
            ls.at[5 + part],
        )
        for part in range(2)
    ]
    for copy in [kcopy, vcopy, qcopy]:
        copy.start()

    spot = lax.broadcasted_iota(jnp.int32, (4, 128), 1)
    dense = jnp.zeros((4, 128), F32)
    for k in range(ids.shape[1]):
        dense = dense + jnp.where(ids[:, k : k + 1] == spot // 2, gates[:, k : k + 1], 0.0)
    named = (dense > 0.0).astype(jnp.int32)
    r0 = named[0:1, :]
    r1_ = r0 + named[1:2, :]
    r2_ = r1_ + named[2:3, :]
    rank = jnp.concatenate([jnp.zeros((1, 128), jnp.int32), r0, r1_, r2_], axis=0)
    table = jnp.where(rank == lax.rem(spot, 2), dense, 0.0)
    gsend[...] = jnp.concatenate([table, table], axis=0)
    gbuf[e] = gsend[...]

    greet([(1, cn, ctx), (1, en, exp)])

    def qpush(j):
        return remote(q, qbuf.at[c], qs.at[j], qr.at[c], ctx(j))

    loop(cn, lambda j: qpush(j).start(), start=1)

    def gpush(j):
        return remote(gsend, gbuf.at[e], gs.at[j], gr.at[e], exp(j))

    loop(en, lambda j: gpush(j).start(), start=1)

    def wpush(part):
        off = pl.multiple_of(part * 2 * half + (1 - h) * half, 128)
        return remote(
            w.at[:, :, pl.ds(off, half)],
            wbuf.at[:, h, :, pl.ds(part * half, half)],
            ws.at[part],
            wr.at[part],
            (other, e),
        )

    wpush(0).start()
    wpush(1).start()
    kcopy.wait()
    vcopy.wait()
    qcopy.wait()
    for copy in wcopies + [owcopy, wdcopy]:
        copy.start()
    vt[...] = vbuf[...].astype(F32).T.astype(BF16)
    mbuf[...] = jnp.full(mbuf.shape, NEG, F32)
    scale = 1.0 / math.sqrt(HD)
    scale2 = scale * math.log2(math.e)
    first_q = key_rows * cn - rows * cn
    kc = min(512, key_rows)

    def opush(j):
        cs = csrc(j)
        return remote(osend.at[cs], obuf.at[c], os_.at[j], or_.at[c], (cs, e))

    def spush(j):
        cs = csrc(j)
        return remote(stsend.at[cs], stbuf.at[c], ss.at[j], sr.at[c], (cs, e))

    def osend_start(j):
        spush(j).start()
        opush(j).start()

    def attend(j):
        cs = csrc(j)

        @pl.when(j > 0)
        def _():
            remote(q, qbuf.at[cs], qs.at[0], qr.at[cs], (cs, e)).wait_recv()

        @pl.when(j > 1)
        def _():
            osend_start(j - 1)

        qv = qbuf[cs]
        qcat = jnp.concatenate([qv[:, i * HD : (i + 1) * HD] for i in range(heads)], axis=0)
        for t in range(key_rows // kc):
            sbuf[t * kc : (t + 1) * kc, :] = lax.dot_general(
                kbuf[t * kc : (t + 1) * kc, :],
                qcat,
                (((1,), (1,)), ((), ())),
                preferred_element_type=F32,
            )

        @pl.when(c == cn - 1)
        def _():
            lane = lax.rem(lax.broadcasted_iota(jnp.int32, (1, cols), 1), rows)
            limit = first_q + cs * rows + lane - c * key_rows
            for t in range(key_rows // kc):
                kpos = t * kc + lax.broadcasted_iota(jnp.int32, (kc, cols), 0)
                sbuf[t * kc : (t + 1) * kc, :] = jnp.where(
                    kpos <= limit, sbuf[t * kc : (t + 1) * kc, :], NEG
                )

        m = jnp.max(sbuf[0:kc, :], axis=0, keepdims=True)
        for t in range(1, key_rows // kc):
            m = jnp.maximum(m, jnp.max(sbuf[t * kc : (t + 1) * kc, :], axis=0, keepdims=True))
        total = jnp.zeros((1, cols), F32)
        acc = jnp.zeros((HD, cols), F32)
        for t in range(key_rows // kc):
            p = jnp.exp2((sbuf[t * kc : (t + 1) * kc, :] - m) * scale2)
            total = total + jnp.sum(p, axis=0, keepdims=True)
            acc = acc + jnp.dot(
                vt[:, t * kc : (t + 1) * kc], p.astype(BF16), preferred_element_type=F32
            )
        got = acc.T.astype(BF16)
        for i in range(heads):
            osend[cs, :, i * HD : (i + 1) * HD] = got[i * rows : (i + 1) * rows, :]
        msc = m * scale
        stsend[cs, 0:1, :hc] = msc[:, :hc]
        stsend[cs, 1:2, :hc] = msc[:, hc:]
        stsend[cs, 2:3, :hc] = total[:, :hc]
        stsend[cs, 3:4, :hc] = total[:, hc:]
        mbuf[0:1, :] = jnp.maximum(mbuf[0:1, :], msc)

    loop(cn, attend)
    hmsend[0:1, :hc] = mbuf[0:1, :hc]
    hmsend[1:2, :hc] = mbuf[0:1, hc:]

    def garrive(j):
        e2 = esrc(j)
        remote(gsend, gbuf.at[e2], gs.at[j], gr.at[e2], (c, e2)).wait_recv()

    loop(en, garrive, start=1)
    osend_start(cn - 1)
    gr_ = lax.broadcasted_iota(jnp.int32, (128, 128), 0)
    gc_ = lax.broadcasted_iota(jnp.int32, (128, 128), 1)
    pick = (gr_ == 4 * e + lax.rem(gc_, 4)).astype(F32)
    picked = jnp.dot(
        gbuf[...].reshape(8 * en, 128), pick, preferred_element_type=F32,
        precision=lax.Precision.HIGHEST,
    )
    picked = jnp.where(gr_[: 8 * en] // 8 == gc_[: 8 * en] // 4, picked, 0.0)
    gpsend[...] = jnp.sum(picked.reshape(en, 8, 128), axis=0)
    gall[c] = gpsend[...]
    obuf[c] = osend[c]
    stbuf[c] = stsend[c]
    hmbuf[c] = hmsend[...]

    def sarrive(j):
        c2 = csrc(j)
        remote(stsend.at[c2], stbuf.at[c2], ss.at[j], sr.at[c2], (c2, e)).wait_recv()

    def oarrive(j):
        c2 = csrc(j)
        remote(osend.at[c2], obuf.at[c2], os_.at[j], or_.at[c2], (c2, e)).wait_recv()

    loop(cn, sarrive, start=1)
    peak = functools.reduce(jnp.maximum, [stbuf[i, 0:2, :] for i in range(cn)])
    weights = [jnp.exp(stbuf[i, 0:2, :] - peak) for i in range(cn)]
    total = sum(wt * stbuf[i, 2:4, :] for i, wt in enumerate(weights))
    coef[...] = jnp.zeros(coef.shape, F32)
    for i in range(cn):
        coef[2 * i : 2 * i + 2, :] = weights[i] / total
    turned = coef[...].T
    dup = (
        lax.broadcasted_iota(jnp.int32, (2 * rows, rows), 1)
        == lax.broadcasted_iota(jnp.int32, (2 * rows, rows), 0) // 8 * 4
        + lax.rem(lax.broadcasted_iota(jnp.int32, (2 * rows, rows), 0), 4)
    ).astype(BF16)
    loop(cn, oarrive, start=1)
    for i in range(heads):
        lo = (i % (heads // 2)) * rows
        acc = jnp.zeros((rows, HD), F32)
        for k in range(cn):
            at = 2 * k + i // (heads // 2)
            acc = acc + turned[lo : lo + rows, at : at + 1] * obuf[
                k, :, i * HD : (i + 1) * HD
            ].astype(F32)
        a2[:, i * HD : (i + 1) * HD] = jnp.dot(
            dup, acc.astype(BF16), preferred_element_type=F32
        ).astype(BF16)
    owcopy.wait()
    left = a2[...]
    nc = min(256, n)
    low = lax.rem(lax.broadcasted_iota(jnp.int32, (2 * rows, nc), 0), 8) < 4

    def column(t):
        at = pl.multiple_of(t * nc, nc)
        v0 = jnp.dot(left, owbuf[:, pl.ds(at, nc)], preferred_element_type=F32)
        v1 = jnp.dot(left, owbuf[:, pl.ds(at + n, nc)], preferred_element_type=F32)
        v = jnp.where(low, v0, v1)
        for k in range(en):
            psend[k, :, pl.ds(at, nc)] = v[8 * k : 8 * k + 8, :].astype(BF16)

    loop(n // nc, column)

    def ppush(j):
        e2 = lax.rem(e + j, en)
        return remote(psend.at[e2], pbuf.at[e], ps.at[j], pr.at[e], (c, e2))

    def parrive(j):
        e2 = esrc(j)
        remote(psend.at[e2], pbuf.at[e2], ps.at[j], pr.at[e2], (c, e2)).wait_recv()

    loop(en, lambda j: ppush(j).start(), start=1)

    def gppush(j):
        return remote(gpsend, gall.at[c], gps.at[j], gpr.at[c], ctx(j))

    def gparrive(j):
        c2 = csrc(j)
        remote(gpsend, gall.at[c2], gps.at[j], gpr.at[c2], (c2, e)).wait_recv()

    def hmpush(j):
        return remote(hmsend, hmbuf.at[c], ms.at[j], mr.at[c], ctx(j))

    def hmarrive(j):
        c2 = csrc(j)
        remote(hmsend, hmbuf.at[c2], ms.at[j], mr.at[c2], (c2, e)).wait_recv()

    loop(cn, lambda j: gppush(j).start(), start=1)
    loop(cn, lambda j: hmpush(j).start(), start=1)
    pbuf[e] = psend[e]
    loop(cn, gparrive, start=1)
    rows_all = gall[...].reshape(lanes, 128)

    def tables(g):
        spread, same, same_half = slot_gates(cn, rows_all, g)
        slotm[g] = jnp.where(same & same_half & (spread > 0.0), 1.0, 0.0).T.astype(BF16)
        part = jnp.where(same, spread, 0.0)
        hi = part.astype(BF16).astype(F32)
        first = lax.broadcasted_iota(jnp.int32, (lanes, lanes), 1) < lanes // 2
        gatem[g] = jnp.where(first, hi, part - hi).astype(BF16)

    loop(en, tables)
    loop(en, parrive, start=1)
    s = sum(pbuf[i].astype(F32) for i in range(en))
    s0 = s[0:4, :] + residual[:, :n].astype(F32)
    s1 = s[4:8, :] + residual[:, n:].astype(F32)
    state[:, :n] = s0
    state[:, n:] = s1
    mean = (
        jnp.sum(s0 * s0, axis=1, keepdims=True) + jnp.sum(s1 * s1, axis=1, keepdims=True)
    ) * (1.0 / d)
    inv = lax.rsqrt(mean + EPS)
    n0 = s0 * inv * gain[:, :n]
    n1 = s1 * inv * gain[:, n:]
    for i in range(cn):
        part, off = (n0, i * 256) if i * 256 < n else (n1, i * 256 - n)
        xsend[i] = jnp.concatenate(
            [part[:, off : off + 128], part[:, off + 128 : off + 256]], axis=0
        ).astype(BF16)

    def xpush(j):
        c2 = lax.rem(c + j, cn)
        return remote(xsend.at[c2], mid.at[c], xsm.at[j], xrm.at[c], (c2, e))

    def xarrive(j):
        c2 = csrc(j)
        remote(xsend.at[c2], mid.at[c2], xsm.at[j], xrm.at[c2], (c2, e)).wait_recv()

    loop(cn, lambda j: xpush(j).start(), start=1)
    mid[c] = xsend[c]
    loop(cn, xarrive, start=1)

    def epush(j):
        return remote(mid, xbuf.at[h, e], es.at[j], er.at[e], exp(j))

    def erelay(j):
        e2 = esrc(j)
        return remote(xbuf.at[h, e2], xbuf.at[h, e2], es2.at[e2], er2.at[e2], (other, e))

    loop(en, lambda j: epush(j).start(), start=1)
    own = remote(mid, xbuf.at[h, e], es2.at[e], er2.at[e], (other, e))
    own.start()
    xbuf[h, e] = mid[...]

    def forward(j):
        e2 = esrc(j)
        remote(mid, xbuf.at[h, e2], es.at[j], er.at[e2], (c, e2)).wait_recv()
        erelay(j).start()

    loop(en, forward, start=1)
    for copy in wcopies:
        copy.wait()
    wpush(0).wait()
    wpush(1).wait()
    sc = 2 * cn
    yc = min(512, 2 * half)

    def ypush(qi, j):
        k = lax.rem(chip + j, nk)
        return remote(
            ysend.at[qi, k], ybuf.at[chip, qi], ys.at[qi, j], yr.at[chip, qi], (k * 2 + h, e)
        )

    def expert_in(qi):
        def group(gl):
            g = qi * gq + gl
            remote(
                xbuf.at[1 - h, g], xbuf.at[1 - h, g], es2.at[g], er2.at[g], (other, e)
            ).wait_recv()
            at = pl.multiple_of(gl * sc, sc)
            for core in range(2):
                xv = xbuf[core, g].astype(F32).reshape(lanes, 128).astype(BF16)
                r = jnp.dot(slotm[g], xv, preferred_element_type=F32).astype(BF16)
                for hf in range(2):
                    for k in range(2):
                        lo = hf * 2 * sc + k * sc
                        f = core * 256 + hf * 128
                        xs[k, pl.ds(at, sc), f : f + 128] = r[lo : lo + sc, :]

        loop(gq, group)
        for x in range(2):
            def ycol(t, x=x):
                at = pl.multiple_of(t * yc, yc)
                r = jnp.dot(
                    xs[x, :, 0:256], wbuf[x, 0, :, pl.ds(at, yc)], preferred_element_type=F32
                )
                r = r + jnp.dot(
                    xs[x, :, 256:512], wbuf[x, 1, :, pl.ds(at, yc)], preferred_element_type=F32
                )
                r = r.astype(BF16)
                for k in range(nk):
                    ysend[qi, k, x, :, pl.ds(at, yc)] = r[k * cn : (k + 1) * cn, :]

            loop(2 * half // yc, ycol)
        loop(nk, lambda j: ypush(qi, j).start(), start=1)

    loop(nq, expert_in)

    def hpush(qi, j):
        k = lax.rem(chip + j, nk)
        slot = hbuf.at[h, chip, qi]
        return remote(slot, slot, hs.at[qi, j], hr.at[chip, qi], (k * 2 + h, e))

    def hrelay(qi, k):
        slot = hbuf.at[h, k, qi]
        return remote(slot, slot, hs2.at[qi, k], hr2.at[k, qi], (other, e))

    def reduce_in(qi):
        def yarrive(j):
            k = lax.rem(chip + nk - j, nk)
            remote(
                ysend.at[qi, k], ybuf.at[k, qi], ys.at[qi, j], yr.at[k, qi], (k * 2 + h, e)
            ).wait_recv()

        ybuf[chip, qi] = ysend[qi, chip]
        loop(nk, yarrive, start=1)
        for x in range(2):
            up = sum(ybuf[k, qi, x, :, half:].astype(F32) for k in range(nk))
            gate = sum(ybuf[k, qi, x, :, 0:half].astype(F32) for k in range(nk))
            hbuf[h, chip, qi, x] = (gate / (1.0 + jnp.exp(-gate)) * up).astype(BF16)
        loop(nk, lambda j: hpush(qi, j).start(), start=1)
        hrelay(qi, chip).start()

    def relay(qi):
        def one(j):
            k = lax.rem(chip + nk - j, nk)
            slot = hbuf.at[h, k, qi]
            remote(slot, slot, hs.at[qi, j], hr.at[k, qi], (k * 2 + h, e)).wait_recv()
            hrelay(qi, k).start()

        loop(nk, one, start=1)

    low128 = lax.rem(lax.broadcasted_iota(jnp.int32, (lanes, 128), 0), 8) < 4

    def cpush(e2):
        return remote(csend.at[e2], r1.at[e], cs_.at[e2], cr_.at[e], (c, e2))

    def expert_out(qi):
        def harrive(k):
            slot = hbuf.at[1 - h, k, qi]
            remote(slot, slot, hs2.at[qi, k], hr2.at[k, qi], (other, e)).wait_recv()

        loop(nk, harrive)
        outs = []
        for x in range(2):
            r = jnp.zeros((nk * cn, 256), F32)
            for hh in range(2):
                left = hbuf[hh, :, qi, x].reshape(nk * cn, half)
                r = r + jnp.dot(
                    left, wdbuf[x, hh * half : (hh + 1) * half, :], preferred_element_type=F32
                )
            outs.append(r.astype(BF16))
        for gl in range(gq):
            g = qi * gq + gl
            ov = [o[gl * sc : (gl + 1) * sc, :] for o in outs]
            ov = jnp.concatenate(ov + ov, axis=0)
            r = jnp.dot(gatem[g], ov, preferred_element_type=F32)
            csend[g] = jnp.where(low128, r[:, :128], r[:, 128:]).reshape(cn, 8, 128).astype(BF16)
        for gl in range(gq):
            g = qi * gq + gl

            @pl.when(g != e)
            def _():
                cpush(g).start()

    wdcopy.wait()
    reduce_in(0)
    for qi in range(1, nq):
        reduce_in(qi)
        relay(qi - 1)
        if qi > 1:
            expert_out(qi - 2)
    relay(nq - 1)
    expert_out(nq - 2)
    expert_out(nq - 1)
    r1[e] = csend[e]

    def carrive(j):
        e2 = esrc(j)
        remote(csend.at[e2], r1.at[e2], cs_.at[e2], cr_.at[e2], (c, e2)).wait_recv()

    loop(cn, hmarrive, start=1)
    top = functools.reduce(jnp.maximum, [hmbuf[i] for i in range(cn)])
    place4 = lax.broadcasted_iota(jnp.int32, (1, heads), 1)
    best = jnp.zeros((1, heads), F32)
    for i in range(heads):
        a, b = i // (heads // 2), i % (heads // 2)
        peak1 = jnp.max(top[a : a + 1, b * rows : (b + 1) * rows], axis=1, keepdims=True)
        best = jnp.where(place4 == i, peak1, best)
    hm[...] = best
    loop(en, carrive, start=1)

    def rpush(j):
        c2 = lax.rem(c + j, cn)
        return remote(r1.at[:, c2], r2.at[c], rs_.at[j], rr_.at[c], (c2, e))

    def rarrive(j):
        c2 = csrc(j)
        remote(r1.at[:, c2], r2.at[c2], rs_.at[j], rr_.at[c2], (c2, e)).wait_recv()

    loop(cn, lambda j: rpush(j).start(), start=1)
    r2[c] = r1[:, c]
    loop(cn, rarrive, start=1)
    for i in range(cn):
        s = sum(r2[i, k].astype(F32) for k in range(en))
        for hf in range(2):
            f = i * 256 + hf * 128
            out[:, f : f + 128] = state[:, f : f + 128] + s[4 * hf : 4 * hf + 4, :]

    for push in (qpush, opush, spush, gppush, hmpush, xpush, rpush):
        loop(cn, lambda j, push=push: push(j).wait_send(), start=1)
    for push in (gpush, ppush, epush, erelay):
        loop(en, lambda j, push=push: push(j).wait_send(), start=1)
    own.wait_send()
    loop(en, lambda j: cpush(lax.rem(e + j, en)).wait_send(), start=1)
    for qi in range(nq):
        loop(nk, lambda j, qi=qi: ypush(qi, j).wait_send(), start=1)
        loop(nk, lambda j, qi=qi: hpush(qi, j).wait_send(), start=1)
        loop(nk, lambda k, qi=qi: hrelay(qi, k).wait_send())


def local(cn, en, query, keys, values, out_weight, residual, norm_gain, expert_ids, gate_values,
          w_gate_up, w_down):
    rows, width = query.shape
    heads = width // HD
    d = out_weight.shape[1]
    key_rows = keys.shape[0]
    cols = rows * heads
    ff = w_down.shape[1]
    half = ff // 2
    fb = w_gate_up.shape[1]
    nk = cn // 2
    gq = cn // 4
    nq = en // gq
    v = pltpu.VMEM
    layer_out, head_max = pl.pallas_call(
        functools.partial(layer_kernel, cn, en),
        out_shape=(
            jax.ShapeDtypeStruct((4, d), F32),
            jax.ShapeDtypeStruct((1, heads), F32),
        ),
        in_specs=[ANY] * 6 + [VM] * 4,
        out_specs=(VM, VM),
        scratch_shapes=[
            v((cn, rows, width), BF16),
            v((key_rows, HD), BF16),
            v((key_rows, HD), BF16),
            v((HD, key_rows), BF16),
            v((key_rows, cols), F32),
            v((8, cols), F32),
            v((cn, rows, width), BF16),
            v((cn, rows, width), BF16),
            v((cn, 8, 128), F32),
            v((cn, 8, 128), F32),
            v((8, 128), F32),
            v((cn, 8, 128), F32),
            v((8, 128), F32),
            v((en, 8, 128), F32),
            v((8, 128), F32),
            v((cn, 8, 128), F32),
            v((width, d), BF16),
            v((128, 128), F32),
            v((2 * rows, width), BF16),
            v((en, 8, d // 2), BF16),
            v((en, 8, d // 2), BF16),
            v((4, d), F32),
            v((cn, 8, 128), BF16),
            v((cn, 8, 128), BF16),
            v((2, en, cn, 8, 128), BF16),
            v((2, 2, fb, ff), BF16),
            v((en, 8 * cn, 8 * cn), BF16),
            v((en, 8 * cn, 8 * cn), BF16),
            v((2, gq * 2 * cn, 2 * fb), BF16),
            v((nq, nk, 2, cn, ff), BF16),
            v((nk, nq, 2, cn, ff), BF16),
            v((2, nk, nq, 2, cn, half), BF16),
            v((2, ff, fb), BF16),
            v((en, cn, 8, 128), BF16),
            v((en, cn, 8, 128), BF16),
            v((cn, en, 8, 128), BF16),
            DMA((cn,)), DMA((cn,)), DMA((cn,)), DMA((cn,)), DMA((cn,)), DMA((cn,)),
            DMA((cn,)), DMA((cn,)), DMA((en,)), DMA((en,)), DMA((cn,)), DMA((cn,)),
            DMA((2,)), DMA((2,)), DMA((en,)), DMA((en,)), DMA((cn,)), DMA((cn,)),
            DMA((en,)), DMA((en,)), DMA((en,)), DMA((en,)),
            DMA((nq, nk)), DMA((nk, nq)), DMA((nq, nk)), DMA((nk, nq)),
            DMA((nq, nk)), DMA((nk, nq)),
            DMA((en,)), DMA((en,)), DMA((cn,)), DMA((cn,)), DMA((7,)),
        ],
        compiler_params=pltpu.CompilerParams(
            collective_id=0, has_side_effects=True, vmem_limit_bytes=60 << 20
        ),
        name="layer_kernel",
    )(
        query, keys, values, w_gate_up, out_weight, w_down, expert_ids, gate_values, residual,
        norm_gain.reshape(1, d),
    )
    return layer_out, head_max.reshape(heads)


def solution(mesh):
    cn, en = mesh.shape["ctx"], mesh.shape["exp"]
    return jax.shard_map(
        functools.partial(local, cn, en),
        mesh=mesh,
        in_specs=(
            P("ctx", "exp"),
            P("ctx", None),
            P("ctx", None),
            P("exp", None),
            P(("ctx", "exp"), None),
            P(),
            P(("ctx", "exp"), None),
            P(("ctx", "exp"), None),
            P("exp", "ctx", None),
            P("exp", None, "ctx"),
        ),
        out_specs=(P(("ctx", "exp"), None), P("exp")),
        check_vma=False,
    )
```

```python
import functools
import math

import jax
import jax.numpy as jnp
from jax import lax
from jax.experimental import pallas as pl
from jax.experimental.pallas import tpu as pltpu
from jax.sharding import PartitionSpec as P

HEADS = 64
KVH = 4
HD = 128
EPS = 1e-06
NEG = -1e30
MESH = pl.DeviceIdType.MESH
ANY = pl.BlockSpec(memory_space=pl.ANY)
VM = pl.BlockSpec(memory_space=pltpu.VMEM)
F32 = jnp.float32
BF16 = jnp.bfloat16
DMA = pltpu.SemaphoreType.DMA


def loop(n, body, start=0):
    def step(i, carry):
        body(i)
        return carry

    lax.fori_loop(start, n, step, 0)


def place(cn, en):
    return lax.axis_index("ctx"), lax.axis_index("exp")


def greet(targets):
    barrier = pltpu.get_barrier_semaphore()
    total = 0
    for first, last, device in targets:
        loop(
            last,
            lambda j, device=device: pl.semaphore_signal(
                barrier, inc=1, device_id=device(j), device_id_type=MESH
            ),
            start=first,
        )
        total += last - first
    pl.semaphore_wait(barrier, total)


def remote(src, dst, send, recv, device):
    return pltpu.make_async_remote_copy(
        src_ref=src,
        dst_ref=dst,
        send_sem=send,
        recv_sem=recv,
        device_id=device,
        device_id_type=MESH,
    )


def slot_gates(cn, gall, group):
    lanes = 8 * cn
    row = lax.broadcasted_iota(jnp.int32, (lanes, lanes), 0)
    col = lax.broadcasted_iota(jnp.int32, (lanes, lanes), 1)
    k = lax.broadcasted_iota(jnp.int32, (128, lanes), 0)
    which = lax.rem(lax.broadcasted_iota(jnp.int32, (128, lanes), 1) // cn, 4)
    pick = (k == 4 * group + which).astype(F32)
    spread = jnp.dot(gall, pick, preferred_element_type=F32, precision=lax.Precision.HIGHEST)
    same = row // 8 == lax.rem(col, cn)
    same_half = lax.rem(row // 4, 2) == col // (4 * cn)
    return spread, same, same_half


def layer_kernel(cn, en, q, keys, vals, w, outw, wd, ids, gates, residual, gain, out, hm,
                 qbuf, kbuf, vbuf, vt, sbuf, mbuf, osend, obuf, stsend, stbuf, hmsend, hmbuf,
                 gsend, gbuf, gpsend, gall, owbuf, coef, a2, psend, pbuf, state, xsend, mid, xbuf,
                 wbuf, slotm, gatem, xs, ysend, ybuf, hbuf, wdbuf, csend, r1, r2,
                 qs, qr, os_, or_, ss, sr, ms, mr, gs, gr, gps, gpr, ws, wr, ps, pr, xsm, xrm,
                 es, er, es2, er2, ys, yr, hs, hr, hs2, hr2, cs_, cr_, rs_, rr_, ls):
    c, e = place(cn, en)
    h = lax.rem(c, 2)
    other = c + 1 - 2 * h
    chip = c // 2
    nk = cn // 2
    gq = cn // 4
    nq = en // gq
    rows, width = q.shape
    heads = width // HD
    key_rows = keys.shape[0]
    half = w.shape[2] // 4
    cols = heads * rows
    hc = cols // 2
    lanes = 8 * cn
    d = outw.shape[1]
    n = d // 2

    def ctx(j):
        return (lax.rem(c + j, cn), e)

    def exp(j):
        return (c, lax.rem(e + j, en))

    def csrc(j):
        return lax.rem(c + cn - j, cn)

    def esrc(j):
        return lax.rem(e + en - j, en)

    kv = pl.multiple_of((e * heads // (HEADS // KVH)) * HD, HD)
    kcopy = pltpu.make_async_copy(keys.at[:, pl.ds(kv, HD)], kbuf, ls.at[0])
    vcopy = pltpu.make_async_copy(vals.at[:, pl.ds(kv, HD)], vbuf, ls.at[1])
    qcopy = pltpu.make_async_copy(q, qbuf.at[c], ls.at[2])
    owcopy = pltpu.make_async_copy(outw, owbuf, ls.at[3])
    wdcopy = pltpu.make_async_copy(wd, wdbuf, ls.at[4])
    wcopies = [
        pltpu.make_async_copy(
            w.at[:, :, pl.ds(pl.multiple_of(part * 2 * half + h * half, 128), half)],
            wbuf.at[:, h, :, pl.ds(part * half, half)],
            ls.at[5 + part],
        )
        for part in range(2)
    ]
    for copy in [kcopy, vcopy, qcopy]:
        copy.start()

    spot = lax.broadcasted_iota(jnp.int32, (4, 128), 1)
    dense = jnp.zeros((4, 128), F32)
    for k in range(ids.shape[1]):
        dense = dense + jnp.where(ids[:, k : k + 1] == spot // 2, gates[:, k : k + 1], 0.0)
    named = (dense > 0.0).astype(jnp.int32)
    r0 = named[0:1, :]
    r1_ = r0 + named[1:2, :]
    r2_ = r1_ + named[2:3, :]
    rank = jnp.concatenate([jnp.zeros((1, 128), jnp.int32), r0, r1_, r2_], axis=0)
    table = jnp.where(rank == lax.rem(spot, 2), dense, 0.0)
    gsend[...] = jnp.concatenate([table, table], axis=0)
    gbuf[e] = gsend[...]

    greet([(1, cn, ctx), (1, en, exp)])

    def asrc(j):
        k = lax.rem(chip + nk - j // 2, nk)
        return 2 * k + jnp.where(lax.rem(j, 2) == 0, h, 1 - h)

    def qpush(m):
        return remote(q, qbuf.at[c], qs.at[m], qr.at[c], (lax.rem(chip + m, nk) * 2 + h, e))

    qpair = remote(q, qbuf.at[c], qs.at[0], qr.at[c], (other, e))

    def qrelay(m):
        cs = asrc(2 * m)
        return remote(qbuf.at[cs], qbuf.at[cs], qs.at[nk + m], qr.at[cs], (other, e))

    qpair.start()
    loop(nk, lambda m: qpush(m).start(), start=1)

    def gpush(j):
        return remote(gsend, gbuf.at[e], gs.at[j], gr.at[e], exp(j))

    loop(en, lambda j: gpush(j).start(), start=1)

    def wpush(part):
        off = pl.multiple_of(part * 2 * half + (1 - h) * half, 128)
        return remote(
            w.at[:, :, pl.ds(off, half)],
            wbuf.at[:, h, :, pl.ds(part * half, half)],
            ws.at[part],
            wr.at[part],
            (other, e),
        )

    wpush(0).start()
    wpush(1).start()
    kcopy.wait()
    vcopy.wait()
    qcopy.wait()
    for copy in wcopies + [owcopy, wdcopy]:
        copy.start()
    vt[...] = vbuf[...].astype(F32).T.astype(BF16)
    mbuf[...] = jnp.full(mbuf.shape, NEG, F32)
    scale = 1.0 / math.sqrt(HD)
    scale2 = scale * math.log2(math.e)
    first_q = key_rows * cn - rows * cn
    kc = min(512, key_rows)

    def opush(j):
        cs = asrc(j)
        return remote(osend.at[cs], obuf.at[c], os_.at[j], or_.at[c], (cs, e))

    def spush(j):
        cs = asrc(j)
        return remote(stsend.at[cs], stbuf.at[c], ss.at[j], sr.at[c], (cs, e))

    def osend_start(j):
        spush(j).start()
        opush(j).start()

    def attend(j):
        cs = asrc(j)

        @pl.when(j > 0)
        def _():
            remote(q, qbuf.at[cs], qs.at[0], qr.at[cs], (cs, e)).wait_recv()

        @pl.when((j > 0) & (lax.rem(j, 2) == 0))
        def _():
            qrelay(j // 2).start()

        @pl.when(j > 1)
        def _():
            osend_start(j - 1)

        qv = qbuf[cs]
        qcat = jnp.concatenate([qv[:, i * HD : (i + 1) * HD] for i in range(heads)], axis=0)
        for t in range(key_rows // kc):
            sbuf[t * kc : (t + 1) * kc, :] = lax.dot_general(
                kbuf[t * kc : (t + 1) * kc, :],
                qcat,
                (((1,), (1,)), ((), ())),
                preferred_element_type=F32,
            )

        @pl.when(c == cn - 1)
        def _():
            lane = lax.rem(lax.broadcasted_iota(jnp.int32, (1, cols), 1), rows)
            limit = first_q + cs * rows + lane - c * key_rows
            for t in range(key_rows // kc):
                kpos = t * kc + lax.broadcasted_iota(jnp.int32, (kc, cols), 0)
                sbuf[t * kc : (t + 1) * kc, :] = jnp.where(
                    kpos <= limit, sbuf[t * kc : (t + 1) * kc, :], NEG
                )

        m = jnp.max(sbuf[0:kc, :], axis=0, keepdims=True)
        for t in range(1, key_rows // kc):
            m = jnp.maximum(m, jnp.max(sbuf[t * kc : (t + 1) * kc, :], axis=0, keepdims=True))
        total = jnp.zeros((1, cols), F32)
        acc = jnp.zeros((HD, cols), F32)
        for t in range(key_rows // kc):
            p = jnp.exp2((sbuf[t * kc : (t + 1) * kc, :] - m) * scale2)
            total = total + jnp.sum(p, axis=0, keepdims=True)
            acc = acc + jnp.dot(
                vt[:, t * kc : (t + 1) * kc], p.astype(BF16), preferred_element_type=F32
            )
        got = acc.T.astype(BF16)
        for i in range(heads):
            osend[cs, :, i * HD : (i + 1) * HD] = got[i * rows : (i + 1) * rows, :]
        msc = m * scale
        stsend[cs, 0:1, :hc] = msc[:, :hc]
        stsend[cs, 1:2, :hc] = msc[:, hc:]
        stsend[cs, 2:3, :hc] = total[:, :hc]
        stsend[cs, 3:4, :hc] = total[:, hc:]
        mbuf[0:1, :] = jnp.maximum(mbuf[0:1, :], msc)

    loop(cn, attend)
    hmsend[0:1, :hc] = mbuf[0:1, :hc]
    hmsend[1:2, :hc] = mbuf[0:1, hc:]

    def garrive(j):
        e2 = esrc(j)
        remote(gsend, gbuf.at[e2], gs.at[j], gr.at[e2], (c, e2)).wait_recv()

    loop(en, garrive, start=1)
    osend_start(cn - 1)
    gr_ = lax.broadcasted_iota(jnp.int32, (128, 128), 0)
    gc_ = lax.broadcasted_iota(jnp.int32, (128, 128), 1)
    pick = (gr_ == 4 * e + lax.rem(gc_, 4)).astype(F32)
    picked = jnp.dot(
        gbuf[...].reshape(8 * en, 128), pick, preferred_element_type=F32,
        precision=lax.Precision.HIGHEST,
    )
    picked = jnp.where(gr_[: 8 * en] // 8 == gc_[: 8 * en] // 4, picked, 0.0)
    gpsend[...] = jnp.sum(picked.reshape(en, 8, 128), axis=0)
    gall[c] = gpsend[...]
    obuf[c] = osend[c]
    stbuf[c] = stsend[c]
    hmbuf[c] = hmsend[...]

    def sarrive(j):
        c2 = csrc(j)
        remote(stsend.at[c2], stbuf.at[c2], ss.at[j], sr.at[c2], (c2, e)).wait_recv()

    def oarrive(j):
        c2 = csrc(j)
        remote(osend.at[c2], obuf.at[c2], os_.at[j], or_.at[c2], (c2, e)).wait_recv()

    loop(cn, sarrive, start=1)
    peak = functools.reduce(jnp.maximum, [stbuf[i, 0:2, :] for i in range(cn)])
    weights = [jnp.exp(stbuf[i, 0:2, :] - peak) for i in range(cn)]
    total = sum(wt * stbuf[i, 2:4, :] for i, wt in enumerate(weights))
    coef[...] = jnp.zeros(coef.shape, F32)
    for i in range(cn):
        coef[2 * i : 2 * i + 2, :] = weights[i] / total
    turned = coef[...].T
    dup = (
        lax.broadcasted_iota(jnp.int32, (2 * rows, rows), 1)
        == lax.broadcasted_iota(jnp.int32, (2 * rows, rows), 0) // 8 * 4
        + lax.rem(lax.broadcasted_iota(jnp.int32, (2 * rows, rows), 0), 4)
    ).astype(BF16)
    loop(cn, oarrive, start=1)
    for i in range(heads):
        lo = (i % (heads // 2)) * rows
        acc = jnp.zeros((rows, HD), F32)
        for k in range(cn):
            at = 2 * k + i // (heads // 2)
            acc = acc + turned[lo : lo + rows, at : at + 1] * obuf[
                k, :, i * HD : (i + 1) * HD
            ].astype(F32)
        a2[:, i * HD : (i + 1) * HD] = jnp.dot(
            dup, acc.astype(BF16), preferred_element_type=F32
        ).astype(BF16)
    owcopy.wait()
    left = a2[...]
    nc = min(256, n)
    low = lax.rem(lax.broadcasted_iota(jnp.int32, (2 * rows, nc), 0), 8) < 4

    def column(t):
        at = pl.multiple_of(t * nc, nc)
        v0 = jnp.dot(left, owbuf[:, pl.ds(at, nc)], preferred_element_type=F32)
        v1 = jnp.dot(left, owbuf[:, pl.ds(at + n, nc)], preferred_element_type=F32)
        v = jnp.where(low, v0, v1)
        for k in range(en):
            psend[k, :, pl.ds(at, nc)] = v[8 * k : 8 * k + 8, :].astype(BF16)

    loop(n // nc, column)

    def ppush(j):
        e2 = lax.rem(e + j, en)
        return remote(psend.at[e2], pbuf.at[e], ps.at[j], pr.at[e], (c, e2))

    def parrive(j):
        e2 = esrc(j)
        remote(psend.at[e2], pbuf.at[e2], ps.at[j], pr.at[e2], (c, e2)).wait_recv()

    loop(en, lambda j: ppush(j).start(), start=1)

    def gppush(j):
        return remote(gpsend, gall.at[c], gps.at[j], gpr.at[c], ctx(j))

    def gparrive(j):
        c2 = csrc(j)
        remote(gpsend, gall.at[c2], gps.at[j], gpr.at[c2], (c2, e)).wait_recv()

    def hmpush(j):
        return remote(hmsend, hmbuf.at[c], ms.at[j], mr.at[c], ctx(j))

    def hmarrive(j):
        c2 = csrc(j)
        remote(hmsend, hmbuf.at[c2], ms.at[j], mr.at[c2], (c2, e)).wait_recv()

    loop(cn, lambda j: gppush(j).start(), start=1)
    loop(cn, lambda j: hmpush(j).start(), start=1)
    pbuf[e] = psend[e]
    loop(cn, gparrive, start=1)
    rows_all = gall[...].reshape(lanes, 128)

    def tables(g):
        spread, same, same_half = slot_gates(cn, rows_all, g)
        slotm[g] = jnp.where(same & same_half & (spread > 0.0), 1.0, 0.0).T.astype(BF16)
        part = jnp.where(same, spread, 0.0)
        hi = part.astype(BF16).astype(F32)
        first = lax.broadcasted_iota(jnp.int32, (lanes, lanes), 1) < lanes // 2
        gatem[g] = jnp.where(first, hi, part - hi).astype(BF16)

    loop(en, tables)
    loop(en, parrive, start=1)
    s = sum(pbuf[i].astype(F32) for i in range(en))
    s0 = s[0:4, :] + residual[:, :n].astype(F32)
    s1 = s[4:8, :] + residual[:, n:].astype(F32)
    state[:, :n] = s0
    state[:, n:] = s1
    mean = (
        jnp.sum(s0 * s0, axis=1, keepdims=True) + jnp.sum(s1 * s1, axis=1, keepdims=True)
    ) * (1.0 / d)
    inv = lax.rsqrt(mean + EPS)
    n0 = s0 * inv * gain[:, :n]
    n1 = s1 * inv * gain[:, n:]
    for i in range(cn):
        part, off = (n0, i * 256) if i * 256 < n else (n1, i * 256 - n)
        xsend[i] = jnp.concatenate(
            [part[:, off : off + 128], part[:, off + 128 : off + 256]], axis=0
        ).astype(BF16)

    def xpush(j):
        c2 = lax.rem(c + j, cn)
        return remote(xsend.at[c2], mid.at[c], xsm.at[j], xrm.at[c], (c2, e))

    def xarrive(j):
        c2 = csrc(j)
        remote(xsend.at[c2], mid.at[c2], xsm.at[j], xrm.at[c2], (c2, e)).wait_recv()

    loop(cn, lambda j: xpush(j).start(), start=1)
    mid[c] = xsend[c]
    loop(cn, xarrive, start=1)

    def epush(j):
        return remote(mid, xbuf.at[h, e], es.at[j], er.at[e], exp(j))

    def erelay(j):
        e2 = esrc(j)
        return remote(xbuf.at[h, e2], xbuf.at[h, e2], es2.at[e2], er2.at[e2], (other, e))

    loop(en, lambda j: epush(j).start(), start=1)
    own = remote(mid, xbuf.at[h, e], es2.at[e], er2.at[e], (other, e))
    own.start()
    xbuf[h, e] = mid[...]

    def forward(j):
        e2 = esrc(j)
        remote(mid, xbuf.at[h, e2], es.at[j], er.at[e2], (c, e2)).wait_recv()
        erelay(j).start()

    loop(en, forward, start=1)
    for copy in wcopies:
        copy.wait()
    wpush(0).wait()
    wpush(1).wait()
    sc = 2 * cn
    yc = min(512, 2 * half)

    def ypush(qi, j):
        k = lax.rem(chip + j, nk)
        return remote(
            ysend.at[qi, k], ybuf.at[chip, qi], ys.at[qi, j], yr.at[chip, qi], (k * 2 + h, e)
        )

    def expert_in(qi):
        def group(gl):
            g = qi * gq + gl
            remote(
                xbuf.at[1 - h, g], xbuf.at[1 - h, g], es2.at[g], er2.at[g], (other, e)
            ).wait_recv()
            at = pl.multiple_of(gl * sc, sc)
            for core in range(2):
                xv = xbuf[core, g].astype(F32).reshape(lanes, 128).astype(BF16)
                r = jnp.dot(slotm[g], xv, preferred_element_type=F32).astype(BF16)
                for hf in range(2):
                    for k in range(2):
                        lo = hf * 2 * sc + k * sc
                        f = core * 256 + hf * 128
                        xs[k, pl.ds(at, sc), f : f + 128] = r[lo : lo + sc, :]

        loop(gq, group)
        for x in range(2):
            def ycol(t, x=x):
                at = pl.multiple_of(t * yc, yc)
                r = jnp.dot(
                    xs[x, :, 0:256], wbuf[x, 0, :, pl.ds(at, yc)], preferred_element_type=F32
                )
                r = r + jnp.dot(
                    xs[x, :, 256:512], wbuf[x, 1, :, pl.ds(at, yc)], preferred_element_type=F32
                )
                r = r.astype(BF16)
                for k in range(nk):
                    ysend[qi, k, x, :, pl.ds(at, yc)] = r[k * cn : (k + 1) * cn, :]

            loop(2 * half // yc, ycol)
        loop(nk, lambda j: ypush(qi, j).start(), start=1)

    loop(nq, expert_in)

    def hpush(qi, j):
        k = lax.rem(chip + j, nk)
        slot = hbuf.at[h, chip, qi]
        return remote(slot, slot, hs.at[qi, j], hr.at[chip, qi], (k * 2 + h, e))

    def hrelay(qi, k):
        slot = hbuf.at[h, k, qi]
        return remote(slot, slot, hs2.at[qi, k], hr2.at[k, qi], (other, e))

    def reduce_in(qi):
        def yarrive(j):
            k = lax.rem(chip + nk - j, nk)
            remote(
                ysend.at[qi, k], ybuf.at[k, qi], ys.at[qi, j], yr.at[k, qi], (k * 2 + h, e)
            ).wait_recv()

        ybuf[chip, qi] = ysend[qi, chip]
        loop(nk, yarrive, start=1)
        for x in range(2):
            up = sum(ybuf[k, qi, x, :, half:].astype(F32) for k in range(nk))
            gate = sum(ybuf[k, qi, x, :, 0:half].astype(F32) for k in range(nk))
            hbuf[h, chip, qi, x] = (gate / (1.0 + jnp.exp(-gate)) * up).astype(BF16)
        loop(nk, lambda j: hpush(qi, j).start(), start=1)
        hrelay(qi, chip).start()

    def relay(qi):
        def one(j):
            k = lax.rem(chip + nk - j, nk)
            slot = hbuf.at[h, k, qi]
            remote(slot, slot, hs.at[qi, j], hr.at[k, qi], (k * 2 + h, e)).wait_recv()
            hrelay(qi, k).start()

        loop(nk, one, start=1)

    low128 = lax.rem(lax.broadcasted_iota(jnp.int32, (lanes, 128), 0), 8) < 4

    def cpush(e2):
        return remote(csend.at[e2], r1.at[e], cs_.at[e2], cr_.at[e], (c, e2))

    def expert_out(qi):
        def harrive(k):
            slot = hbuf.at[1 - h, k, qi]
            remote(slot, slot, hs2.at[qi, k], hr2.at[k, qi], (other, e)).wait_recv()

        loop(nk, harrive)
        outs = []
        for x in range(2):
            r = jnp.zeros((nk * cn, 256), F32)
            for hh in range(2):
                left = hbuf[hh, :, qi, x].reshape(nk * cn, half)
                r = r + jnp.dot(
                    left, wdbuf[x, hh * half : (hh + 1) * half, :], preferred_element_type=F32
                )
            outs.append(r.astype(BF16))
        for gl in range(gq):
            g = qi * gq + gl
            ov = [o[gl * sc : (gl + 1) * sc, :] for o in outs]
            ov = jnp.concatenate(ov + ov, axis=0)
            r = jnp.dot(gatem[g], ov, preferred_element_type=F32)
            csend[g] = jnp.where(low128, r[:, :128], r[:, 128:]).reshape(cn, 8, 128).astype(BF16)
        for gl in range(gq):
            g = qi * gq + gl

            @pl.when(g != e)
            def _():
                cpush(g).start()

    wdcopy.wait()
    reduce_in(0)
    for qi in range(1, nq):
        reduce_in(qi)
        relay(qi - 1)
        if qi > 1:
            expert_out(qi - 2)
    relay(nq - 1)
    expert_out(nq - 2)
    expert_out(nq - 1)
    r1[e] = csend[e]

    def carrive(j):
        e2 = esrc(j)
        remote(csend.at[e2], r1.at[e2], cs_.at[e2], cr_.at[e2], (c, e2)).wait_recv()

    loop(cn, hmarrive, start=1)
    top = functools.reduce(jnp.maximum, [hmbuf[i] for i in range(cn)])
    place4 = lax.broadcasted_iota(jnp.int32, (1, heads), 1)
    best = jnp.zeros((1, heads), F32)
    for i in range(heads):
        a, b = i // (heads // 2), i % (heads // 2)
        peak1 = jnp.max(top[a : a + 1, b * rows : (b + 1) * rows], axis=1, keepdims=True)
        best = jnp.where(place4 == i, peak1, best)
    hm[...] = best
    loop(en, carrive, start=1)

    def rpush(j):
        c2 = lax.rem(c + j, cn)
        return remote(r1.at[:, c2], r2.at[c], rs_.at[j], rr_.at[c], (c2, e))

    def rarrive(j):
        c2 = csrc(j)
        remote(r1.at[:, c2], r2.at[c2], rs_.at[j], rr_.at[c2], (c2, e)).wait_recv()

    loop(cn, lambda j: rpush(j).start(), start=1)
    r2[c] = r1[:, c]
    loop(cn, rarrive, start=1)
    for i in range(cn):
        s = sum(r2[i, k].astype(F32) for k in range(en))
        for hf in range(2):
            f = i * 256 + hf * 128
            out[:, f : f + 128] = state[:, f : f + 128] + s[4 * hf : 4 * hf + 4, :]

    qpair.wait_send()
    for push in (qpush, qrelay):
        loop(nk, lambda m, push=push: push(m).wait_send(), start=1)
    for push in (opush, spush, gppush, hmpush, xpush, rpush):
        loop(cn, lambda j, push=push: push(j).wait_send(), start=1)
    for push in (gpush, ppush, epush, erelay):
        loop(en, lambda j, push=push: push(j).wait_send(), start=1)
    own.wait_send()
    loop(en, lambda j: cpush(lax.rem(e + j, en)).wait_send(), start=1)
    for qi in range(nq):
        loop(nk, lambda j, qi=qi: ypush(qi, j).wait_send(), start=1)
        loop(nk, lambda j, qi=qi: hpush(qi, j).wait_send(), start=1)
        loop(nk, lambda k, qi=qi: hrelay(qi, k).wait_send())


def local(cn, en, query, keys, values, out_weight, residual, norm_gain, expert_ids, gate_values,
          w_gate_up, w_down):
    rows, width = query.shape
    heads = width // HD
    d = out_weight.shape[1]
    key_rows = keys.shape[0]
    cols = rows * heads
    ff = w_down.shape[1]
    half = ff // 2
    fb = w_gate_up.shape[1]
    nk = cn // 2
    gq = cn // 4
    nq = en // gq
    v = pltpu.VMEM
    layer_out, head_max = pl.pallas_call(
        functools.partial(layer_kernel, cn, en),
        out_shape=(
            jax.ShapeDtypeStruct((4, d), F32),
            jax.ShapeDtypeStruct((1, heads), F32),
        ),
        in_specs=[ANY] * 6 + [VM] * 4,
        out_specs=(VM, VM),
        scratch_shapes=[
            v((cn, rows, width), BF16),
            v((key_rows, HD), BF16),
            v((key_rows, HD), BF16),
            v((HD, key_rows), BF16),
            v((key_rows, cols), F32),
            v((8, cols), F32),
            v((cn, rows, width), BF16),
            v((cn, rows, width), BF16),
            v((cn, 8, 128), F32),
            v((cn, 8, 128), F32),
            v((8, 128), F32),
            v((cn, 8, 128), F32),
            v((8, 128), F32),
            v((en, 8, 128), F32),
            v((8, 128), F32),
            v((cn, 8, 128), F32),
            v((width, d), BF16),
            v((128, 128), F32),
            v((2 * rows, width), BF16),
            v((en, 8, d // 2), BF16),
            v((en, 8, d // 2), BF16),
            v((4, d), F32),
            v((cn, 8, 128), BF16),
            v((cn, 8, 128), BF16),
            v((2, en, cn, 8, 128), BF16),
            v((2, 2, fb, ff), BF16),
            v((en, 8 * cn, 8 * cn), BF16),
            v((en, 8 * cn, 8 * cn), BF16),
            v((2, gq * 2 * cn, 2 * fb), BF16),
            v((nq, nk, 2, cn, ff), BF16),
            v((nk, nq, 2, cn, ff), BF16),
            v((2, nk, nq, 2, cn, half), BF16),
            v((2, ff, fb), BF16),
            v((en, cn, 8, 128), BF16),
            v((en, cn, 8, 128), BF16),
            v((cn, en, 8, 128), BF16),
            DMA((cn,)), DMA((cn,)), DMA((cn,)), DMA((cn,)), DMA((cn,)), DMA((cn,)),
            DMA((cn,)), DMA((cn,)), DMA((en,)), DMA((en,)), DMA((cn,)), DMA((cn,)),
            DMA((2,)), DMA((2,)), DMA((en,)), DMA((en,)), DMA((cn,)), DMA((cn,)),
            DMA((en,)), DMA((en,)), DMA((en,)), DMA((en,)),
            DMA((nq, nk)), DMA((nk, nq)), DMA((nq, nk)), DMA((nk, nq)),
            DMA((nq, nk)), DMA((nk, nq)),
            DMA((en,)), DMA((en,)), DMA((cn,)), DMA((cn,)), DMA((7,)),
        ],
        compiler_params=pltpu.CompilerParams(
            collective_id=0, has_side_effects=True, vmem_limit_bytes=60 << 20
        ),
        name="layer_kernel",
    )(
        query, keys, values, w_gate_up, out_weight, w_down, expert_ids, gate_values, residual,
        norm_gain.reshape(1, d),
    )
    return layer_out, head_max.reshape(heads)


def solution(mesh):
    cn, en = mesh.shape["ctx"], mesh.shape["exp"]
    return jax.shard_map(
        functools.partial(local, cn, en),
        mesh=mesh,
        in_specs=(
            P("ctx", "exp"),
            P("ctx", None),
            P("ctx", None),
            P("exp", None),
            P(("ctx", "exp"), None),
            P(),
            P(("ctx", "exp"), None),
            P(("ctx", "exp"), None),
            P("exp", "ctx", None),
            P("exp", None, "ctx"),
        ),
        out_specs=(P(("ctx", "exp"), None), P("exp")),
        check_vma=False,
    )
```

```python
import functools
import math

import jax
import jax.numpy as jnp
from jax import lax
from jax.experimental import pallas as pl
from jax.experimental.pallas import tpu as pltpu
from jax.sharding import PartitionSpec as P

HEADS = 64
KVH = 4
HD = 128
EPS = 1e-06
NEG = -1e30
MESH = pl.DeviceIdType.MESH
ANY = pl.BlockSpec(memory_space=pl.ANY)
VM = pl.BlockSpec(memory_space=pltpu.VMEM)
F32 = jnp.float32
BF16 = jnp.bfloat16
DMA = pltpu.SemaphoreType.DMA


def loop(n, body, start=0):
    def step(i, carry):
        body(i)
        return carry

    lax.fori_loop(start, n, step, 0)


def place(cn, en):
    return lax.axis_index("ctx"), lax.axis_index("exp")


def greet(targets):
    barrier = pltpu.get_barrier_semaphore()
    total = 0
    for first, last, device in targets:
        loop(
            last,
            lambda j, device=device: pl.semaphore_signal(
                barrier, inc=1, device_id=device(j), device_id_type=MESH
            ),
            start=first,
        )
        total += last - first
    pl.semaphore_wait(barrier, total)


def remote(src, dst, send, recv, device):
    return pltpu.make_async_remote_copy(
        src_ref=src,
        dst_ref=dst,
        send_sem=send,
        recv_sem=recv,
        device_id=device,
        device_id_type=MESH,
    )


def slot_gates(cn, gall, group):
    lanes = 8 * cn
    row = lax.broadcasted_iota(jnp.int32, (lanes, lanes), 0)
    col = lax.broadcasted_iota(jnp.int32, (lanes, lanes), 1)
    k = lax.broadcasted_iota(jnp.int32, (128, lanes), 0)
    which = lax.rem(lax.broadcasted_iota(jnp.int32, (128, lanes), 1) // cn, 4)
    pick = (k == 4 * group + which).astype(F32)
    spread = jnp.dot(gall, pick, preferred_element_type=F32, precision=lax.Precision.HIGHEST)
    same = row // 8 == lax.rem(col, cn)
    same_half = lax.rem(row // 4, 2) == col // (4 * cn)
    return spread, same, same_half


def layer_kernel(cn, en, q, keys, vals, w, outw, wd, ids, gates, residual, gain, out, hm,
                 qbuf, kbuf, vbuf, vt, sbuf, mbuf, osend, obuf, stsend, stbuf, hmsend, hmbuf,
                 gsend, gbuf, gpsend, gall, owbuf, coef, a2, psend, pbuf, state, xsend, mid, xbuf,
                 wbuf, slotm, gatem, xs, ysend, ybuf, hbuf, wdbuf, csend, r1, rsum, r2,
                 qs, qr, os_, or_, ss, sr, ms, mr, gs, gr, gps, gpr, ws, wr, ps, pr, xsm, xrm,
                 es, er, es2, er2, ys, yr, hs, hr, hs2, hr2, cs_, cr_, rs_, rr_, ls):
    c, e = place(cn, en)
    h = lax.rem(c, 2)
    other = c + 1 - 2 * h
    chip = c // 2
    nk = cn // 2
    gq = cn // 4
    nq = en // gq
    rows, width = q.shape
    heads = width // HD
    key_rows = keys.shape[0]
    half = w.shape[2] // 4
    cols = heads * rows
    hc = cols // 2
    lanes = 8 * cn
    d = outw.shape[1]
    n = d // 2

    def ctx(j):
        return (lax.rem(c + j, cn), e)

    def exp(j):
        return (c, lax.rem(e + j, en))

    def csrc(j):
        return lax.rem(c + cn - j, cn)

    def esrc(j):
        return lax.rem(e + en - j, en)

    kv = pl.multiple_of((e * heads // (HEADS // KVH)) * HD, HD)
    kcopy = pltpu.make_async_copy(keys.at[:, pl.ds(kv, HD)], kbuf, ls.at[0])
    vcopy = pltpu.make_async_copy(vals.at[:, pl.ds(kv, HD)], vbuf, ls.at[1])
    qcopy = pltpu.make_async_copy(q, qbuf.at[c], ls.at[2])
    owcopy = pltpu.make_async_copy(outw, owbuf, ls.at[3])
    wdcopy = pltpu.make_async_copy(wd, wdbuf, ls.at[4])
    wcopies = [
        pltpu.make_async_copy(
            w.at[:, :, pl.ds(pl.multiple_of(part * 2 * half + h * half, 128), half)],
            wbuf.at[:, h, :, pl.ds(part * half, half)],
            ls.at[5 + part],
        )
        for part in range(2)
    ]
    for copy in [kcopy, vcopy, qcopy]:
        copy.start()

    spot = lax.broadcasted_iota(jnp.int32, (4, 128), 1)
    dense = jnp.zeros((4, 128), F32)
    for k in range(ids.shape[1]):
        dense = dense + jnp.where(ids[:, k : k + 1] == spot // 2, gates[:, k : k + 1], 0.0)
    named = (dense > 0.0).astype(jnp.int32)
    r0 = named[0:1, :]
    r1_ = r0 + named[1:2, :]
    r2_ = r1_ + named[2:3, :]
    rank = jnp.concatenate([jnp.zeros((1, 128), jnp.int32), r0, r1_, r2_], axis=0)
    table = jnp.where(rank == lax.rem(spot, 2), dense, 0.0)
    gsend[...] = jnp.concatenate([table, table], axis=0)
    gbuf[e] = gsend[...]

    greet([(1, cn, ctx), (1, en, exp)])

    def asrc(j):
        k = lax.rem(chip + nk - j // 2, nk)
        return 2 * k + jnp.where(lax.rem(j, 2) == 0, h, 1 - h)

    def qpush(m):
        return remote(q, qbuf.at[c], qs.at[m], qr.at[c], (lax.rem(chip + m, nk) * 2 + h, e))

    qpair = remote(q, qbuf.at[c], qs.at[0], qr.at[c], (other, e))

    def qrelay(m):
        cs = asrc(2 * m)
        return remote(qbuf.at[cs], qbuf.at[cs], qs.at[nk + m], qr.at[cs], (other, e))

    qpair.start()
    loop(nk, lambda m: qpush(m).start(), start=1)

    def gpush(j):
        return remote(gsend, gbuf.at[e], gs.at[j], gr.at[e], exp(j))

    loop(en, lambda j: gpush(j).start(), start=1)

    def wpush(part):
        off = pl.multiple_of(part * 2 * half + (1 - h) * half, 128)
        return remote(
            w.at[:, :, pl.ds(off, half)],
            wbuf.at[:, h, :, pl.ds(part * half, half)],
            ws.at[part],
            wr.at[part],
            (other, e),
        )

    wpush(0).start()
    wpush(1).start()
    kcopy.wait()
    vcopy.wait()
    qcopy.wait()
    for copy in wcopies + [owcopy, wdcopy]:
        copy.start()
    vt[...] = vbuf[...].astype(F32).T.astype(BF16)
    mbuf[...] = jnp.full(mbuf.shape, NEG, F32)
    scale = 1.0 / math.sqrt(HD)
    scale2 = scale * math.log2(math.e)
    first_q = key_rows * cn - rows * cn
    kc = min(512, key_rows)

    def opush(j):
        cs = asrc(j)
        return remote(osend.at[cs], obuf.at[c], os_.at[j], or_.at[c], (cs, e))

    def spush(j):
        cs = asrc(j)
        return remote(stsend.at[cs], stbuf.at[c], ss.at[j], sr.at[c], (cs, e))

    def osend_start(j):
        spush(j).start()
        opush(j).start()

    def attend(j):
        cs = asrc(j)

        @pl.when(j > 0)
        def _():
            remote(q, qbuf.at[cs], qs.at[0], qr.at[cs], (cs, e)).wait_recv()

        @pl.when((j > 0) & (lax.rem(j, 2) == 0))
        def _():
            qrelay(j // 2).start()

        @pl.when(j > 1)
        def _():
            osend_start(j - 1)

        qv = qbuf[cs]
        qcat = jnp.concatenate([qv[:, i * HD : (i + 1) * HD] for i in range(heads)], axis=0)
        for t in range(key_rows // kc):
            sbuf[t * kc : (t + 1) * kc, :] = lax.dot_general(
                kbuf[t * kc : (t + 1) * kc, :],
                qcat,
                (((1,), (1,)), ((), ())),
                preferred_element_type=F32,
            )

        @pl.when(c == cn - 1)
        def _():
            lane = lax.rem(lax.broadcasted_iota(jnp.int32, (1, cols), 1), rows)
            limit = first_q + cs * rows + lane - c * key_rows
            for t in range(key_rows // kc):
                kpos = t * kc + lax.broadcasted_iota(jnp.int32, (kc, cols), 0)
                sbuf[t * kc : (t + 1) * kc, :] = jnp.where(
                    kpos <= limit, sbuf[t * kc : (t + 1) * kc, :], NEG
                )

        m = jnp.max(sbuf[0:kc, :], axis=0, keepdims=True)
        for t in range(1, key_rows // kc):
            m = jnp.maximum(m, jnp.max(sbuf[t * kc : (t + 1) * kc, :], axis=0, keepdims=True))
        total = jnp.zeros((1, cols), F32)
        acc = jnp.zeros((HD, cols), F32)
        for t in range(key_rows // kc):
            p = jnp.exp2((sbuf[t * kc : (t + 1) * kc, :] - m) * scale2)
            total = total + jnp.sum(p, axis=0, keepdims=True)
            acc = acc + jnp.dot(
                vt[:, t * kc : (t + 1) * kc], p.astype(BF16), preferred_element_type=F32
            )
        got = acc.T.astype(BF16)
        for i in range(heads):
            osend[cs, :, i * HD : (i + 1) * HD] = got[i * rows : (i + 1) * rows, :]
        msc = m * scale
        stsend[cs, 0:1, :hc] = msc[:, :hc]
        stsend[cs, 1:2, :hc] = msc[:, hc:]
        stsend[cs, 2:3, :hc] = total[:, :hc]
        stsend[cs, 3:4, :hc] = total[:, hc:]
        mbuf[0:1, :] = jnp.maximum(mbuf[0:1, :], msc)

    loop(cn, attend)
    hmsend[0:1, :hc] = mbuf[0:1, :hc]
    hmsend[1:2, :hc] = mbuf[0:1, hc:]

    def garrive(j):
        e2 = esrc(j)
        remote(gsend, gbuf.at[e2], gs.at[j], gr.at[e2], (c, e2)).wait_recv()

    loop(en, garrive, start=1)
    osend_start(cn - 1)
    gr_ = lax.broadcasted_iota(jnp.int32, (128, 128), 0)
    gc_ = lax.broadcasted_iota(jnp.int32, (128, 128), 1)
    pick = (gr_ == 4 * e + lax.rem(gc_, 4)).astype(F32)
    picked = jnp.dot(
        gbuf[...].reshape(8 * en, 128), pick, preferred_element_type=F32,
        precision=lax.Precision.HIGHEST,
    )
    picked = jnp.where(gr_[: 8 * en] // 8 == gc_[: 8 * en] // 4, picked, 0.0)
    gpsend[...] = jnp.sum(picked.reshape(en, 8, 128), axis=0)
    gall[c] = gpsend[...]
    obuf[c] = osend[c]
    stbuf[c] = stsend[c]
    hmbuf[c] = hmsend[...]

    def sarrive(j):
        c2 = csrc(j)
        remote(stsend.at[c2], stbuf.at[c2], ss.at[j], sr.at[c2], (c2, e)).wait_recv()

    def oarrive(j):
        c2 = csrc(j)
        remote(osend.at[c2], obuf.at[c2], os_.at[j], or_.at[c2], (c2, e)).wait_recv()

    loop(cn, sarrive, start=1)
    peak = functools.reduce(jnp.maximum, [stbuf[i, 0:2, :] for i in range(cn)])
    weights = [jnp.exp(stbuf[i, 0:2, :] - peak) for i in range(cn)]
    total = sum(wt * stbuf[i, 2:4, :] for i, wt in enumerate(weights))
    coef[...] = jnp.zeros(coef.shape, F32)
    for i in range(cn):
        coef[2 * i : 2 * i + 2, :] = weights[i] / total
    turned = coef[...].T
    dup = (
        lax.broadcasted_iota(jnp.int32, (2 * rows, rows), 1)
        == lax.broadcasted_iota(jnp.int32, (2 * rows, rows), 0) // 8 * 4
        + lax.rem(lax.broadcasted_iota(jnp.int32, (2 * rows, rows), 0), 4)
    ).astype(BF16)
    loop(cn, oarrive, start=1)
    for i in range(heads):
        lo = (i % (heads // 2)) * rows
        acc = jnp.zeros((rows, HD), F32)
        for k in range(cn):
            at = 2 * k + i // (heads // 2)
            acc = acc + turned[lo : lo + rows, at : at + 1] * obuf[
                k, :, i * HD : (i + 1) * HD
            ].astype(F32)
        a2[:, i * HD : (i + 1) * HD] = jnp.dot(
            dup, acc.astype(BF16), preferred_element_type=F32
        ).astype(BF16)
    owcopy.wait()
    left = a2[...]
    nc = min(256, n)
    low = lax.rem(lax.broadcasted_iota(jnp.int32, (2 * rows, nc), 0), 8) < 4

    def column(t):
        at = pl.multiple_of(t * nc, nc)
        v0 = jnp.dot(left, owbuf[:, pl.ds(at, nc)], preferred_element_type=F32)
        v1 = jnp.dot(left, owbuf[:, pl.ds(at + n, nc)], preferred_element_type=F32)
        v = jnp.where(low, v0, v1)
        for k in range(en):
            psend[k, :, pl.ds(at, nc)] = v[8 * k : 8 * k + 8, :].astype(BF16)

    loop(n // nc, column)

    def ppush(j):
        e2 = lax.rem(e + j, en)
        return remote(psend.at[e2], pbuf.at[e], ps.at[j], pr.at[e], (c, e2))

    def parrive(j):
        e2 = esrc(j)
        remote(psend.at[e2], pbuf.at[e2], ps.at[j], pr.at[e2], (c, e2)).wait_recv()

    loop(en, lambda j: ppush(j).start(), start=1)

    def gppush(j):
        return remote(gpsend, gall.at[c], gps.at[j], gpr.at[c], ctx(j))

    def gparrive(j):
        c2 = csrc(j)
        remote(gpsend, gall.at[c2], gps.at[j], gpr.at[c2], (c2, e)).wait_recv()

    def hmpush(j):
        return remote(hmsend, hmbuf.at[c], ms.at[j], mr.at[c], ctx(j))

    def hmarrive(j):
        c2 = csrc(j)
        remote(hmsend, hmbuf.at[c2], ms.at[j], mr.at[c2], (c2, e)).wait_recv()

    loop(cn, lambda j: gppush(j).start(), start=1)
    loop(cn, lambda j: hmpush(j).start(), start=1)
    pbuf[e] = psend[e]
    loop(cn, gparrive, start=1)
    rows_all = gall[...].reshape(lanes, 128)

    def tables(g):
        spread, same, same_half = slot_gates(cn, rows_all, g)
        slotm[g] = jnp.where(same & same_half & (spread > 0.0), 1.0, 0.0).T.astype(BF16)
        part = jnp.where(same, spread, 0.0)
        hi = part.astype(BF16).astype(F32)
        first = lax.broadcasted_iota(jnp.int32, (lanes, lanes), 1) < lanes // 2
        gatem[g] = jnp.where(first, hi, part - hi).astype(BF16)

    loop(en, tables)
    loop(en, parrive, start=1)
    s = sum(pbuf[i].astype(F32) for i in range(en))
    s0 = s[0:4, :] + residual[:, :n].astype(F32)
    s1 = s[4:8, :] + residual[:, n:].astype(F32)
    state[:, :n] = s0
    state[:, n:] = s1
    mean = (
        jnp.sum(s0 * s0, axis=1, keepdims=True) + jnp.sum(s1 * s1, axis=1, keepdims=True)
    ) * (1.0 / d)
    inv = lax.rsqrt(mean + EPS)
    n0 = s0 * inv * gain[:, :n]
    n1 = s1 * inv * gain[:, n:]
    for i in range(cn):
        part, off = (n0, i * 256) if i * 256 < n else (n1, i * 256 - n)
        xsend[i] = jnp.concatenate(
            [part[:, off : off + 128], part[:, off + 128 : off + 256]], axis=0
        ).astype(BF16)

    def xpush(j):
        c2 = lax.rem(c + j, cn)
        return remote(xsend.at[c2], mid.at[c], xsm.at[j], xrm.at[c], (c2, e))

    def xarrive(j):
        c2 = csrc(j)
        remote(xsend.at[c2], mid.at[c2], xsm.at[j], xrm.at[c2], (c2, e)).wait_recv()

    loop(cn, lambda j: xpush(j).start(), start=1)
    mid[c] = xsend[c]
    loop(cn, xarrive, start=1)

    def epush(j):
        return remote(mid, xbuf.at[h, e], es.at[j], er.at[e], exp(j))

    def erelay(j):
        e2 = esrc(j)
        return remote(xbuf.at[h, e2], xbuf.at[h, e2], es2.at[e2], er2.at[e2], (other, e))

    loop(en, lambda j: epush(j).start(), start=1)
    own = remote(mid, xbuf.at[h, e], es2.at[e], er2.at[e], (other, e))
    own.start()
    xbuf[h, e] = mid[...]

    def forward(j):
        e2 = esrc(j)
        remote(mid, xbuf.at[h, e2], es.at[j], er.at[e2], (c, e2)).wait_recv()
        erelay(j).start()

    loop(en, forward, start=1)
    for copy in wcopies:
        copy.wait()
    wpush(0).wait()
    wpush(1).wait()
    sc = 2 * cn
    yc = min(512, 2 * half)

    def ypush(qi, j):
        k = lax.rem(chip + j, nk)
        return remote(
            ysend.at[qi, k], ybuf.at[chip, qi], ys.at[qi, j], yr.at[chip, qi], (k * 2 + h, e)
        )

    def expert_in(qi):
        def group(gl):
            g = qi * gq + gl
            remote(
                xbuf.at[1 - h, g], xbuf.at[1 - h, g], es2.at[g], er2.at[g], (other, e)
            ).wait_recv()
            at = pl.multiple_of(gl * sc, sc)
            for core in range(2):
                xv = xbuf[core, g].astype(F32).reshape(lanes, 128).astype(BF16)
                r = jnp.dot(slotm[g], xv, preferred_element_type=F32).astype(BF16)
                for hf in range(2):
                    for k in range(2):
                        lo = hf * 2 * sc + k * sc
                        f = core * 256 + hf * 128
                        xs[k, pl.ds(at, sc), f : f + 128] = r[lo : lo + sc, :]

        loop(gq, group)
        for x in range(2):
            def ycol(t, x=x):
                at = pl.multiple_of(t * yc, yc)
                r = jnp.dot(
                    xs[x, :, 0:256], wbuf[x, 0, :, pl.ds(at, yc)], preferred_element_type=F32
                )
                r = r + jnp.dot(
                    xs[x, :, 256:512], wbuf[x, 1, :, pl.ds(at, yc)], preferred_element_type=F32
                )
                r = r.astype(BF16)
                for k in range(nk):
                    ysend[qi, k, x, :, pl.ds(at, yc)] = r[k * cn : (k + 1) * cn, :]

            loop(2 * half // yc, ycol)
        loop(nk, lambda j: ypush(qi, j).start(), start=1)

    loop(nq, expert_in)

    def hpush(qi, j):
        k = lax.rem(chip + j, nk)
        slot = hbuf.at[h, chip, qi]
        return remote(slot, slot, hs.at[qi, j], hr.at[chip, qi], (k * 2 + h, e))

    def hrelay(qi, k):
        slot = hbuf.at[h, k, qi]
        return remote(slot, slot, hs2.at[qi, k], hr2.at[k, qi], (other, e))

    def reduce_in(qi):
        def yarrive(j):
            k = lax.rem(chip + nk - j, nk)
            remote(
                ysend.at[qi, k], ybuf.at[k, qi], ys.at[qi, j], yr.at[k, qi], (k * 2 + h, e)
            ).wait_recv()

        ybuf[chip, qi] = ysend[qi, chip]
        loop(nk, yarrive, start=1)
        for x in range(2):
            up = sum(ybuf[k, qi, x, :, half:].astype(F32) for k in range(nk))
            gate = sum(ybuf[k, qi, x, :, 0:half].astype(F32) for k in range(nk))
            hbuf[h, chip, qi, x] = (gate / (1.0 + jnp.exp(-gate)) * up).astype(BF16)
        loop(nk, lambda j: hpush(qi, j).start(), start=1)
        hrelay(qi, chip).start()

    def relay(qi):
        def one(j):
            k = lax.rem(chip + nk - j, nk)
            slot = hbuf.at[h, k, qi]
            remote(slot, slot, hs.at[qi, j], hr.at[k, qi], (k * 2 + h, e)).wait_recv()
            hrelay(qi, k).start()

        loop(nk, one, start=1)

    low128 = lax.rem(lax.broadcasted_iota(jnp.int32, (lanes, 128), 0), 8) < 4

    def cpush(e2):
        return remote(csend.at[e2], r1.at[e], cs_.at[e2], cr_.at[e], (c, e2))

    def expert_out(qi):
        def harrive(k):
            slot = hbuf.at[1 - h, k, qi]
            remote(slot, slot, hs2.at[qi, k], hr2.at[k, qi], (other, e)).wait_recv()

        loop(nk, harrive)
        outs = []
        for x in range(2):
            r = jnp.zeros((nk * cn, 256), F32)
            for hh in range(2):
                left = hbuf[hh, :, qi, x].reshape(nk * cn, half)
                r = r + jnp.dot(
                    left, wdbuf[x, hh * half : (hh + 1) * half, :], preferred_element_type=F32
                )
            outs.append(r.astype(BF16))
        for gl in range(gq):
            g = qi * gq + gl
            ov = [o[gl * sc : (gl + 1) * sc, :] for o in outs]
            ov = jnp.concatenate(ov + ov, axis=0)
            r = jnp.dot(gatem[g], ov, preferred_element_type=F32)
            csend[g] = jnp.where(low128, r[:, :128], r[:, 128:]).reshape(cn, 8, 128).astype(BF16)
        for gl in range(gq):
            g = qi * gq + gl

            @pl.when(g != e)
            def _():
                cpush(g).start()

    wdcopy.wait()
    reduce_in(0)
    for qi in range(1, nq):
        reduce_in(qi)
        relay(qi - 1)
        if qi > 1:
            expert_out(qi - 2)
    relay(nq - 1)
    expert_out(nq - 2)
    expert_out(nq - 1)
    r1[e] = csend[e]

    def carrive(j):
        e2 = esrc(j)
        remote(csend.at[e2], r1.at[e2], cs_.at[e2], cr_.at[e2], (c, e2)).wait_recv()

    loop(cn, hmarrive, start=1)
    top = functools.reduce(jnp.maximum, [hmbuf[i] for i in range(cn)])
    place4 = lax.broadcasted_iota(jnp.int32, (1, heads), 1)
    best = jnp.zeros((1, heads), F32)
    for i in range(heads):
        a, b = i // (heads // 2), i % (heads // 2)
        peak1 = jnp.max(top[a : a + 1, b * rows : (b + 1) * rows], axis=1, keepdims=True)
        best = jnp.where(place4 == i, peak1, best)
    hm[...] = best
    loop(en, carrive, start=1)

    def rpush(j):
        c2 = lax.rem(c + j, cn)
        return remote(rsum.at[c2], r2.at[c], rs_.at[j], rr_.at[c], (c2, e))

    def rarrive(j):
        c2 = csrc(j)
        remote(rsum.at[c2], r2.at[c2], rs_.at[j], rr_.at[c2], (c2, e)).wait_recv()

    for i in range(cn):
        rsum[i] = sum(r1[k, i].astype(F32) for k in range(en))
    loop(cn, lambda j: rpush(j).start(), start=1)
    r2[c] = rsum[c]
    loop(cn, rarrive, start=1)
    for i in range(cn):
        s = r2[i]
        for hf in range(2):
            f = i * 256 + hf * 128
            out[:, f : f + 128] = state[:, f : f + 128] + s[4 * hf : 4 * hf + 4, :]

    qpair.wait_send()
    for push in (qpush, qrelay):
        loop(nk, lambda m, push=push: push(m).wait_send(), start=1)
    for push in (opush, spush, gppush, hmpush, xpush, rpush):
        loop(cn, lambda j, push=push: push(j).wait_send(), start=1)
    for push in (gpush, ppush, epush, erelay):
        loop(en, lambda j, push=push: push(j).wait_send(), start=1)
    own.wait_send()
    loop(en, lambda j: cpush(lax.rem(e + j, en)).wait_send(), start=1)
    for qi in range(nq):
        loop(nk, lambda j, qi=qi: ypush(qi, j).wait_send(), start=1)
        loop(nk, lambda j, qi=qi: hpush(qi, j).wait_send(), start=1)
        loop(nk, lambda k, qi=qi: hrelay(qi, k).wait_send())


def local(cn, en, query, keys, values, out_weight, residual, norm_gain, expert_ids, gate_values,
          w_gate_up, w_down):
    rows, width = query.shape
    heads = width // HD
    d = out_weight.shape[1]
    key_rows = keys.shape[0]
    cols = rows * heads
    ff = w_down.shape[1]
    half = ff // 2
    fb = w_gate_up.shape[1]
    nk = cn // 2
    gq = cn // 4
    nq = en // gq
    v = pltpu.VMEM
    layer_out, head_max = pl.pallas_call(
        functools.partial(layer_kernel, cn, en),
        out_shape=(
            jax.ShapeDtypeStruct((4, d), F32),
            jax.ShapeDtypeStruct((1, heads), F32),
        ),
        in_specs=[ANY] * 6 + [VM] * 4,
        out_specs=(VM, VM),
        scratch_shapes=[
            v((cn, rows, width), BF16),
            v((key_rows, HD), BF16),
            v((key_rows, HD), BF16),
            v((HD, key_rows), BF16),
            v((key_rows, cols), F32),
            v((8, cols), F32),
            v((cn, rows, width), BF16),
            v((cn, rows, width), BF16),
            v((cn, 8, 128), F32),
            v((cn, 8, 128), F32),
            v((8, 128), F32),
            v((cn, 8, 128), F32),
            v((8, 128), F32),
            v((en, 8, 128), F32),
            v((8, 128), F32),
            v((cn, 8, 128), F32),
            v((width, d), BF16),
            v((128, 128), F32),
            v((2 * rows, width), BF16),
            v((en, 8, d // 2), BF16),
            v((en, 8, d // 2), BF16),
            v((4, d), F32),
            v((cn, 8, 128), BF16),
            v((cn, 8, 128), BF16),
            v((2, en, cn, 8, 128), BF16),
            v((2, 2, fb, ff), BF16),
            v((en, 8 * cn, 8 * cn), BF16),
            v((en, 8 * cn, 8 * cn), BF16),
            v((2, gq * 2 * cn, 2 * fb), BF16),
            v((nq, nk, 2, cn, ff), BF16),
            v((nk, nq, 2, cn, ff), BF16),
            v((2, nk, nq, 2, cn, half), BF16),
            v((2, ff, fb), BF16),
            v((en, cn, 8, 128), BF16),
            v((en, cn, 8, 128), BF16),
            v((cn, 8, 128), F32),
            v((cn, 8, 128), F32),
            DMA((cn,)), DMA((cn,)), DMA((cn,)), DMA((cn,)), DMA((cn,)), DMA((cn,)),
            DMA((cn,)), DMA((cn,)), DMA((en,)), DMA((en,)), DMA((cn,)), DMA((cn,)),
            DMA((2,)), DMA((2,)), DMA((en,)), DMA((en,)), DMA((cn,)), DMA((cn,)),
            DMA((en,)), DMA((en,)), DMA((en,)), DMA((en,)),
            DMA((nq, nk)), DMA((nk, nq)), DMA((nq, nk)), DMA((nk, nq)),
            DMA((nq, nk)), DMA((nk, nq)),
            DMA((en,)), DMA((en,)), DMA((cn,)), DMA((cn,)), DMA((7,)),
        ],
        compiler_params=pltpu.CompilerParams(
            collective_id=0, has_side_effects=True, vmem_limit_bytes=60 << 20
        ),
        name="layer_kernel",
    )(
        query, keys, values, w_gate_up, out_weight, w_down, expert_ids, gate_values, residual,
        norm_gain.reshape(1, d),
    )
    return layer_out, head_max.reshape(heads)


def solution(mesh):
    cn, en = mesh.shape["ctx"], mesh.shape["exp"]
    return jax.shard_map(
        functools.partial(local, cn, en),
        mesh=mesh,
        in_specs=(
            P("ctx", "exp"),
            P("ctx", None),
            P("ctx", None),
            P("exp", None),
            P(("ctx", "exp"), None),
            P(),
            P(("ctx", "exp"), None),
            P(("ctx", "exp"), None),
            P("exp", "ctx", None),
            P("exp", None, "ctx"),
        ),
        out_specs=(P(("ctx", "exp"), None), P("exp")),
        check_vma=False,
    )
```
